32 devices in a mesh: inner: 8 (over y, x, core), outer: 4 (over z).
Axes of the slice: x: 2, y: 2, z: 4, core: 2. Of those that a mesh axis runs over, the one named last changes fastest.
Arguments:
- hidden: bfloat16 [8192, 1152], P(('inner', 'outer')), may hold values from -6 to 6
- latents_now: float32 [32, 16, 256], P(('inner', 'outer')), may hold values from -6 to 6
- latents_next: float32 [32, 16, 256], P(('inner', 'outer')), may hold values from -6.3 to 6.3
- timestep: int32 [1], replicated, may hold values from 3 to 9
- version_tags: int32 [32], P(('inner', 'outer')), may hold values from 0 to 7
- noise_levels: float32 [8], replicated, may hold values from 0.5 to 1
- time_weight: bfloat16 [256, 6912], replicated, may hold values from -0.375 to 0.375
- spatial_qkv: bfloat16 [1152, 3456], replicated, may hold values from -0.1875 to 0.1875
- spatial_out: bfloat16 [1152, 1152], replicated, may hold values from -0.1875 to 0.1875
- temporal_qkv: bfloat16 [1152, 3456], replicated, may hold values from -0.1875 to 0.1875
- temporal_out: bfloat16 [1152, 1152], replicated, may hold values from -0.1875 to 0.1875
- final_weight: bfloat16 [16, 1152], replicated, may hold values from -0.1875 to 0.1875
Outputs:
- log_prob: float32 [32, 256], P(('inner', 'outer'))
- next_mean: float32 [32, 16, 256], P(('inner', 'outer'))
The draws below stay inside these ranges and needn't reach their ends.
Inputs may be any that keep to these rules, and one draw needn't show every extreme that they name: `timestep`: the index k of the denoising step, whose time is k / 10.
All inputs are finite; a program needn't handle non-finite values.
Results may differ from the reference program's by a relative error of at most 0.004.
Values may be sent and summed in bfloat16 or wider, within the bound.
A program may use at most 128 MiB of HBM per device.

```python
import math
import jax
import jax.numpy as jnp
from jax import lax

D = 1152
HEADS = 16
C = 16
FREQ = 256
STEPS = 10
VERSIONS = 8
TPF = 256
FRAMES = 32
TOKENS = 8192


def latent_pair(key):
    first_key = jax.random.fold_in(key, 11)
    second_key = jax.random.fold_in(key, 12)
    shape = (FRAMES, C, TPF)
    current = jnp.clip(jax.random.normal(first_key, shape, jnp.float32), -6.0, 6.0)
    jitter = jnp.clip(jax.random.normal(second_key, shape, jnp.float32), -6.0, 6.0)
    return (current, current + 0.05 * jitter)


def draw_latents_now(key, part):
    return latent_pair(key)[0]


def draw_latents_next(key, part):
    return latent_pair(key)[1]


def place_ends(result, own_key, low, top_value):
    longest = result.shape.index(max(result.shape))
    spots = []
    for shift in (0, 1):
        where = [jax.random.randint(jax.random.fold_in(own_key, axis), (), 0, length) for axis, length in enumerate(result.shape)]
        where[longest] = (where[longest] + shift) % result.shape[longest]
        spots.append(tuple(where))
    return result.at[spots[0]].set(low).at[spots[1]].set(top_value)


def block_levels(rng, dims, shards, smallest, largest):
    loudness = 1.0
    for dim, shards_of in shards:
        draws = jax.random.uniform(jax.random.fold_in(jax.random.fold_in(rng, 6), dim), (shards_of,), jnp.float32, smallest / len(shards), largest / len(shards))
        loudness = loudness * jnp.repeat(jnp.exp(draws), dims[dim] // shards_of).reshape((-1,) + (1,) * (len(dims) - 1 - dim))
    return loudness


def noise(rng, extent, deviation, limit, split=(), kind=jnp.bfloat16):
    array = deviation * jax.random.normal(rng, extent, jnp.float32)
    if split:
        array = array * block_levels(rng, extent, split, -0.22, 0.18)
    return jnp.clip(array, -limit, limit).astype(kind)


def setup_inputs(seed: int = 0) -> dict:
    keys = jax.random.split(jax.random.key(seed), 13)
    hidden = noise(keys[0], (TOKENS, D), 1.0, 6.0, ((0, 32),))
    latents_now = draw_latents_now(jax.random.fold_in(keys[12], 71), 0)
    latents_next = draw_latents_next(jax.random.fold_in(keys[12], 71), 0)
    timestep = jax.random.randint(keys[3], (1,), 3, STEPS).astype(jnp.int32)
    version_tags = place_ends(jax.random.randint(keys[4], (FRAMES,), 0, VERSIONS), jax.random.fold_in(keys[4], 1), 0, VERSIONS - 1).astype(jnp.int32)
    noise_levels = jnp.clip(jnp.exp(jax.random.uniform(keys[5], (VERSIONS,), jnp.float32, math.log(0.5), math.log(1.0))), 0.5, 1.0)
    time_weight = noise(keys[6], (FREQ, 6 * D), FREQ ** -0.5, 0.375)
    spatial_qkv = noise(keys[7], (D, 3 * D), D ** -0.5, 0.1875)
    spatial_out = noise(keys[8], (D, D), D ** -0.5, 0.1875)
    temporal_qkv = noise(keys[9], (D, 3 * D), D ** -0.5, 0.1875)
    temporal_out = noise(keys[10], (D, D), D ** -0.5, 0.1875)
    final_weight = noise(keys[11], (C, D), D ** -0.5, 0.1875)
    return dict(hidden=hidden, latents_now=latents_now, latents_next=latents_next, timestep=timestep, version_tags=version_tags, noise_levels=noise_levels, time_weight=time_weight, spatial_qkv=spatial_qkv, spatial_out=spatial_out, temporal_qkv=temporal_qkv, temporal_out=temporal_out, final_weight=final_weight)


norm_eps = 1e-06

def layer_norm(values):
    average = lax.optimization_barrier(jnp.mean(values, -1, keepdims=True))
    centred = values - average
    variance = lax.optimization_barrier(jnp.mean(centred * centred, -1, keepdims=True))
    return centred * lax.rsqrt(variance + norm_eps)

def head_norm(values):
    return values * lax.rsqrt(lax.optimization_barrier(jnp.mean(values * values, -1, keepdims=True)) + norm_eps)

def modulation(timestep, time_weight):
    half_width = FREQ // 2
    time_value = timestep.astype(jnp.float32) / STEPS
    frequencies = jnp.exp(-math.log(10000.0) * jnp.arange(half_width).astype(jnp.float32) / half_width)
    angles = 1000.0 * time_value[:, None] * frequencies[None, :]
    embedded = jnp.concatenate([jnp.cos(angles), jnp.sin(angles)], 1)
    activated = jax.nn.silu(embedded).astype(jnp.bfloat16)
    return jnp.dot(activated, time_weight, preferred_element_type=jnp.float32)[0]

def heads_of(normed, qkv_weight):
    rows = normed.shape[0]
    head_width = D // HEADS
    mixed = jnp.dot(normed, qkv_weight, preferred_element_type=jnp.float32)
    queries = head_norm(mixed[:, :D].reshape(rows, HEADS, head_width)) * head_width ** (-0.5)
    key_rows = head_norm(mixed[:, D:2 * D].reshape(rows, HEADS, head_width))
    value_rows = mixed[:, 2 * D:].reshape(rows, HEADS, head_width)
    return (queries.astype(jnp.bfloat16), key_rows.astype(jnp.bfloat16), value_rows.astype(jnp.bfloat16))

def attend(queries, key_rows, value_rows):
    scores = jnp.einsum('qhe,khe->hqk', queries.astype(jnp.float32), key_rows.astype(jnp.float32))
    weights = jnp.exp(scores)
    weights = (weights / lax.optimization_barrier(jnp.sum(weights, -1, keepdims=True))).astype(jnp.bfloat16)
    mixed = jnp.einsum('hqk,khe->qhe', weights.astype(jnp.float32), value_rows.astype(jnp.float32))
    return mixed.astype(jnp.bfloat16).reshape(queries.shape[0], D)

def reference(hidden, latents_now, latents_next, timestep, version_tags, noise_levels, time_weight, spatial_qkv, spatial_out, temporal_qkv, temporal_out, final_weight):
    table = modulation(timestep, time_weight)
    shift_s = table[0:D]
    scale_s = table[D:2 * D]
    gate_s = table[2 * D:3 * D]
    shift_t = table[3 * D:4 * D]
    scale_t = table[4 * D:5 * D]
    gate_t = table[5 * D:6 * D]
    framed = hidden.reshape(FRAMES, TPF, D)

    def spatial_frame(frame_rows):
        normed = (layer_norm(frame_rows.astype(jnp.float32)) * (1.0 + scale_s) + shift_s).astype(jnp.bfloat16)
        queries, key_rows, value_rows = heads_of(normed, spatial_qkv)
        mixed = attend(queries, key_rows, value_rows)
        projected = jnp.dot(mixed, spatial_out, preferred_element_type=jnp.float32)
        return (frame_rows.astype(jnp.float32) + gate_s * projected).astype(jnp.bfloat16)
    after_spatial = lax.map(spatial_frame, framed)
    columns = jnp.swapaxes(after_spatial, 0, 1)

    def temporal_column(column_rows):
        normed = (layer_norm(column_rows.astype(jnp.float32)) * (1.0 + scale_t) + shift_t).astype(jnp.bfloat16)
        queries, key_rows, value_rows = heads_of(normed, temporal_qkv)
        mixed = attend(queries, key_rows, value_rows)
        return jnp.dot(mixed, temporal_out, preferred_element_type=jnp.float32).astype(jnp.bfloat16)
    temporal_term = jnp.swapaxes(lax.map(temporal_column, columns), 0, 1)
    final_state = after_spatial.astype(jnp.float32) + gate_t * temporal_term.astype(jnp.float32)
    final_normed = layer_norm(final_state).astype(jnp.bfloat16)
    velocity = jnp.einsum('cd,ftd->fct', final_weight.astype(jnp.float32), final_normed.astype(jnp.float32))
    time_value = timestep.astype(jnp.float32)[0] / STEPS
    matches = (version_tags[:, None] == jnp.arange(VERSIONS).astype(jnp.int32)[None, :]).astype(jnp.float32)
    levels = lax.optimization_barrier(jnp.sum(noise_levels[None, :] * matches, 1))
    noise_scale = levels * jnp.sqrt(time_value / (1.0 - time_value))
    factor = (noise_scale * noise_scale / (2.0 * time_value))[:, None, None]
    drift = velocity + factor * (latents_now + (1.0 - time_value) * velocity)
    next_mean = latents_now - drift / STEPS
    spread = noise_scale * math.sqrt(1.0 / STEPS)
    standard = (latents_next - next_mean) / spread[:, None, None]
    log_prob = -0.5 * lax.optimization_barrier(jnp.mean(standard * standard, 1)) - jnp.log(spread)[:, None] - 0.5 * math.log(2.0 * math.pi)
    return (log_prob, next_mean)
```

```python
import functools
import math

import jax
import jax.numpy as jnp
from jax import lax
from jax.experimental import pallas as pl
from jax.experimental.pallas import tpu as pltpu
from jax.sharding import PartitionSpec as P

HEADS = 16
STEPS = 10
LANES = 128
WINDOW = 256
GROUP = 8
norm_eps = 1e-06
f32 = jnp.float32
bf16 = jnp.bfloat16
MESH = pl.DeviceIdType.MESH


def layer_norm(values):
    average = jnp.mean(values, -1, keepdims=True)
    centred = values - average
    variance = jnp.mean(centred * centred, -1, keepdims=True)
    return centred * lax.rsqrt(variance + norm_eps)


def split_pair(values):
    high = values.astype(bf16)
    return high, (values - high.astype(f32)).astype(bf16)


def dot(a, b):
    return jnp.dot(a, b, preferred_element_type=f32)


def dot_t(a, b):
    return lax.dot_general(a, b, (((1,), (1,)), ((), ())), preferred_element_type=f32)


def kernel(
    sizes,
    hidden_hbm,
    now_hbm,
    next_hbm,
    step_ref,
    tag_ref,
    level_ref,
    final_hbm,
    time_hbm,
    sqkv_hbm,
    sout_hbm,
    tqkv_hbm,
    tout_hbm,
    logp_ref,
    mean_ref,
    hidden_ref,
    now_ref,
    next_ref,
    final_ref,
    time_w,
    sqkv_w,
    sout_w,
    tqkv_w,
    tout_w,
    table,
    group_ref,
    spread_ref,
    mask_ref,
    q_ref,
    k_ref,
    v_ref,
    out_buf,
    in_buf,
    back_buf,
    ret_buf,
    w_sem,
    send_sem,
    recv_sem,
    send2_sem,
    recv2_sem,
):
    inner_size, outer_size = sizes
    peers = inner_size * outer_size
    rows, width = hidden_hbm.shape
    count = rows // peers
    head = width // HEADS
    half_peers = peers // 2
    half_rows = rows // 2
    chips = inner_size // 2
    inner = lax.axis_index("inner")
    outer = lax.axis_index("outer")
    core = lax.rem(inner, 2)
    chip = inner // 2
    me = inner * outer_size + outer

    my_block = core * half_peers + chip * outer_size + outer

    far = outer_size // 2 if outer_size % 2 == 0 else 0

    def outer_of(j):
        span = outer_size - far
        side = outer // span
        crossing = (1 - side) * far + lax.rem(outer + j, span)
        same = side * span + lax.rem(outer + j - far, span)
        return jnp.where(j < far, crossing, same)

    def fetch(source, target, index, lo, hi):
        return pltpu.make_async_copy(
            source.at[:, lo:hi], target.at[:, lo:hi], w_sem.at[index]
        )

    loads = [
        fetch(time_hbm, time_w, 0, 0, 2 * width),
        fetch(sqkv_hbm, sqkv_w, 1, 0, width),
        fetch(sqkv_hbm, sqkv_w, 2, width, 2 * width),
        fetch(sqkv_hbm, sqkv_w, 3, 2 * width, 3 * width),
        fetch(time_hbm, time_w, 4, 2 * width, 6 * width),
        fetch(sout_hbm, sout_w, 5, 0, width),
        fetch(tqkv_hbm, tqkv_w, 6, 0, 3 * width),
        fetch(tout_hbm, tout_w, 7, 0, width),
    ]
    rest = [
        pltpu.make_async_copy(now_hbm, now_ref, w_sem.at[9]),
        pltpu.make_async_copy(next_hbm, next_ref, w_sem.at[10]),
        pltpu.make_async_copy(final_hbm, final_ref, w_sem.at[11]),
    ]
    hidden_load = pltpu.make_async_copy(hidden_hbm, hidden_ref, w_sem.at[8])
    loads[0].start()
    hidden_load.start()
    for load in loads[1:4]:
        load.start()

    barrier = pltpu.get_barrier_semaphore()

    @pl.loop(1, peers)
    def _(k):
        peer = lax.rem(me + k, peers)
        pl.semaphore_signal(
            barrier,
            inc=1,
            device_id=(peer // outer_size, lax.rem(peer, outer_size)),
            device_id_type=MESH,
        )

    feature = lax.broadcasted_iota(jnp.int32, (width, LANES), 0)
    column = lax.broadcasted_iota(jnp.int32, (width, LANES), 1) * head
    group_ref[...] = jnp.where(
        (feature >= column) & (feature < column + head), 1.0, 0.0
    ).astype(bf16)
    feature = lax.broadcasted_iota(jnp.int32, (LANES, width), 1)
    column = lax.broadcasted_iota(jnp.int32, (LANES, width), 0) * head
    spread = jnp.where((feature >= column) & (feature < column + head), 1.0, 0.0).astype(bf16)
    spread_ref[0:LANES, :] = spread
    spread_ref[LANES:, :] = spread

    time_value = jnp.full((8, LANES), step_ref[0].astype(f32)) / STEPS
    lane = lax.broadcasted_iota(jnp.int32, (8, LANES), 1).astype(f32)
    angles = 1000.0 * time_value * jnp.exp(-math.log(10000.0) * lane / LANES)
    embedded = jnp.concatenate([jnp.cos(angles), jnp.sin(angles)], 1)
    activated = (embedded / (1.0 + jnp.exp(-embedded))).astype(bf16)
    loads[0].wait()
    loads[5].start()
    loads[4].start()
    table[:, 0 : 2 * width] = dot(activated, time_w[:, 0 : 2 * width])

    def entry(index):
        return table[0:1, index * width : (index + 1) * width]

    hidden_load.wait()
    hidden = hidden_ref[...].astype(f32)
    normed = (layer_norm(hidden) * (1.0 + entry(1)) + entry(0)).astype(bf16)

    def head_norm(values, factor):
        high, low = split_pair(values * values)
        total = dot(high, group_ref[...]) + dot(low, group_ref[...])
        inverse = lax.rsqrt(total / head + norm_eps) * factor
        high, low = split_pair(inverse)
        return (values * dot(jnp.concatenate([high, low], 1), spread_ref[...])).astype(bf16)

    def project(normed, weight, waits):
        waits[0]()
        q_ref[...] = head_norm(dot(normed, weight[:, 0:width]), head**-0.5)
        waits[1]()
        k_ref[...] = head_norm(dot(normed, weight[:, width : 2 * width]), 1.0)
        waits[2]()
        v_ref[...] = dot(normed, weight[:, 2 * width : 3 * width]).astype(bf16)

    def attend(lo, size, masked):
        tiles = width // LANES
        tops, bottoms = [None] * tiles, [None] * tiles
        lane = lax.broadcasted_iota(jnp.int32, (1, WINDOW), 1)

        def window_of(index):
            tile = min(index * head // LANES, (width - WINDOW) // LANES)
            inside = (lane >= index * head - tile * LANES) & (
                lane < (index + 1) * head - tile * LANES
            )
            return tile, jnp.where(inside, 1.0, 0.0).astype(bf16)

        for first in range(0, HEADS, GROUP):
            group = range(first, first + GROUP)
            scores = []
            for index in group:
                tile, own = window_of(index)
                window = slice(tile * LANES, tile * LANES + WINDOW)
                scores.append(dot_t(q_ref[lo : lo + size, window] * own, k_ref[:, window]))
            weights = []
            for score in scores:
                weight = jnp.exp(score).astype(bf16)
                if masked:
                    weight = weight * mask_ref[lo : lo + size, :]
                weights.append(weight)
            for index, weight in zip(group, weights):
                tile, own = window_of(index)
                window = slice(tile * LANES, tile * LANES + WINDOW)
                mixed = dot(weight, v_ref[:, window] * own + (1.0 - own))
                for side in range(WINDOW // LANES):
                    begin = index * head - (tile + side) * LANES
                    if begin >= LANES or begin + head <= 0:
                        continue
                    top = mixed[:, side * LANES : (side + 1) * LANES]
                    bottom = mixed[:, (1 - side) * LANES : (2 - side) * LANES]
                    here = tile + side
                    if tops[here] is None:
                        tops[here], bottoms[here] = top, bottom
                    else:
                        short = lane[:, :LANES] >= begin
                        tops[here] = jnp.where(short, top, tops[here])
                        bottoms[here] = jnp.where(short, bottom, bottoms[here])
        return jnp.concatenate(
            [(top / bottom).astype(bf16) for top, bottom in zip(tops, bottoms)], 1
        )

    project(normed, sqkv_w, [loads[1].wait, loads[2].wait, loads[3].wait])
    loads[6].start()
    loads[7].start()
    for load in rest:
        load.start()
    loads[4].wait()
    table[:, 2 * width : 5 * width] = dot(activated, time_w[:, 2 * width : 5 * width])
    loads[5].wait()

    def forward(block, inner_id, outer_id):
        return pltpu.make_async_remote_copy(
            src_ref=out_buf.at[block],
            dst_ref=in_buf.at[me],
            send_sem=send_sem.at[block],
            recv_sem=recv_sem.at[me],
            device_id=(inner_id, outer_id),
            device_id_type=MESH,
        )

    for part in range(2):
        lo = part * half_rows
        attended = attend(lo, half_rows, False)
        projected = dot(attended, sout_w[...])
        after = hidden_ref[lo : lo + half_rows, :].astype(f32) + entry(2) * projected
        out_buf[part * half_peers : (part + 1) * half_peers] = after.reshape(
            half_peers, count, width
        ).astype(bf16)
        if part == 0:
            pl.semaphore_wait(barrier, peers - 1)

        def send(k):
            to_chip = lax.rem(chip + lax.rem(k, chips), chips)
            to_outer = outer_of(k // chips)
            block = part * half_peers + to_chip * outer_size + to_outer
            forward(block, 2 * to_chip + part, to_outer).start()

        own = far * chips

        @pl.loop(0, own)
        def _(k):
            send(k)

        @pl.loop(own + 1, half_peers)
        def _(k):
            send(k)

        @pl.when(core != part)
        def _():
            send(own)

        @pl.when(core == part)
        def _():
            in_buf[me] = out_buf[my_block]

    place = lax.rem(lax.broadcasted_iota(jnp.int32, (rows, rows), 0), count)
    other = lax.rem(lax.broadcasted_iota(jnp.int32, (rows, rows), 1), count)
    mask_ref[...] = jnp.where(place == other, 1.0, 0.0).astype(bf16)
    table[:, 5 * width :] = dot(activated, time_w[:, 5 * width :])
    loads[6].wait()
    loads[7].wait()
    for load in rest:
        load.wait()

    @pl.loop(1, peers)
    def _(k):
        peer = lax.rem(me + k, peers)
        pltpu.make_async_remote_copy(
            src_ref=out_buf.at[0],
            dst_ref=in_buf.at[peer],
            send_sem=send_sem.at[0],
            recv_sem=recv_sem.at[peer],
            device_id=(inner, outer),
            device_id_type=MESH,
        ).wait_recv()

    after = in_buf[...].astype(f32).reshape(rows, width)
    normed = (layer_norm(after) * (1.0 + entry(4)) + entry(3)).astype(bf16)
    nothing = lambda: None
    project(normed, tqkv_w, [nothing] * 3)
    attended = attend(0, rows, True)
    term = dot(attended, tout_w[...]).astype(bf16).astype(f32)
    after = in_buf[...].astype(f32).reshape(rows, width)
    final_normed = layer_norm(after + entry(5) * term).astype(bf16)
    channels = final_ref.shape[0]
    repeated = jnp.concatenate([final_ref[...]] * (LANES // channels), 0)
    mixed = dot_t(final_normed, repeated)
    slot = lax.rem(lax.broadcasted_iota(jnp.int32, (rows, LANES), 0), count)
    own_slot = slot == lax.broadcasted_iota(jnp.int32, (rows, LANES), 1) // channels
    packed = jnp.sum(jnp.where(own_slot, mixed, 0.0).reshape(peers, count, LANES), 1)
    back_buf[...] = packed.reshape(peers, 1, LANES)

    def send_back(k):
        to_inner = lax.rem(inner + lax.rem(k, inner_size), inner_size)
        to_outer = outer_of(k // inner_size)
        peer = to_inner * outer_size + to_outer
        pltpu.make_async_remote_copy(
            src_ref=back_buf.at[peer],
            dst_ref=ret_buf.at[my_block],
            send_sem=send2_sem.at[peer],
            recv_sem=recv2_sem.at[my_block],
            device_id=(to_inner, to_outer),
            device_id_type=MESH,
        ).start()

    own = far * inner_size

    @pl.loop(0, own)
    def _(k):
        send_back(k)

    @pl.loop(own + 1, peers)
    def _(k):
        send_back(k)

    ret_buf[my_block] = back_buf[me]

    @pl.loop(1, peers)
    def _(k):
        block = lax.rem(my_block + k, peers)
        pltpu.make_async_remote_copy(
            src_ref=back_buf.at[0],
            dst_ref=ret_buf.at[block],
            send_sem=send2_sem.at[0],
            recv_sem=recv2_sem.at[block],
            device_id=(inner, outer),
            device_id_type=MESH,
        ).wait_recv()

    packed = jnp.broadcast_to(ret_buf[...], (peers, count, LANES)).reshape(rows, LANES)
    packed = jnp.where(own_slot, packed, 0.0)
    high = packed.astype(bf16)
    residue = packed - high.astype(f32)
    middle = residue.astype(bf16)
    low = (residue - middle.astype(f32)).astype(bf16)
    lane = lax.broadcasted_iota(jnp.int32, (channels, LANES), 1)
    pick = lax.rem(lane, channels) == lax.broadcasted_iota(jnp.int32, (channels, LANES), 0)
    pick = jnp.where(pick, 1.0, 0.0).astype(bf16)
    velocity = dot_t(pick, high) + dot_t(pick, middle) + dot_t(pick, low)

    level = jnp.float32(0.0)
    for version in range(level_ref.shape[0]):
        level = level + jnp.where(tag_ref[0] == version, level_ref[version], 0.0)
    time_row = jnp.full((1, rows), step_ref[0].astype(f32)) / STEPS
    noise_scale = level * jnp.sqrt(time_row / (1.0 - time_row))
    factor = noise_scale * noise_scale / (2.0 * time_row)
    now = now_ref[0]
    drift = velocity + factor * (now + (1.0 - time_row) * velocity)
    next_mean = now - drift / STEPS
    mean_ref[0] = next_mean
    deviation = noise_scale * math.sqrt(1.0 / STEPS)
    standard = (next_ref[0] - next_mean) / deviation
    logp_ref[...] = (
        -0.5 * jnp.mean(standard * standard, 0, keepdims=True)
        - jnp.log(deviation)
        - 0.5 * math.log(2.0 * math.pi)
    )

    @pl.loop(1, peers)
    def _(k):
        block = lax.rem(my_block + k, peers)
        peer = lax.rem(me + k, peers)
        pltpu.make_async_remote_copy(
            src_ref=out_buf.at[block],
            dst_ref=in_buf.at[0],
            send_sem=send_sem.at[block],
            recv_sem=recv_sem.at[0],
            device_id=(inner, outer),
            device_id_type=MESH,
        ).wait_send()
        pltpu.make_async_remote_copy(
            src_ref=back_buf.at[peer],
            dst_ref=ret_buf.at[0],
            send_sem=send2_sem.at[peer],
            recv_sem=recv2_sem.at[0],
            device_id=(inner, outer),
            device_id_type=MESH,
        ).wait_send()


def shards(sizes, hidden, now, following, step, tags, levels, time_w, sqkv, sout, tqkv, tout, final):
    peers = sizes[0] * sizes[1]
    rows, width = hidden.shape
    count = rows // peers
    vmem = pl.BlockSpec(memory_space=pltpu.VMEM)
    smem = pl.BlockSpec(memory_space=pltpu.SMEM)
    hbm = pl.BlockSpec(memory_space=pl.ANY)
    exchange = pltpu.VMEM((peers, count, width), bf16)
    sems = pltpu.SemaphoreType.DMA((peers,))
    return pl.pallas_call(
        functools.partial(kernel, sizes),
        out_shape=(pltpu.VMEM((1, rows), f32), pltpu.VMEM(now.shape, f32)),
        in_specs=[hbm, hbm, hbm, smem, smem, smem, hbm] + [hbm] * 5,
        out_specs=(vmem, vmem),
        scratch_shapes=[
            pltpu.VMEM(hidden.shape, bf16),
            pltpu.VMEM(now.shape, f32),
            pltpu.VMEM(following.shape, f32),
            pltpu.VMEM(final.shape, bf16),
            pltpu.VMEM(time_w.shape, bf16),
            pltpu.VMEM(sqkv.shape, bf16),
            pltpu.VMEM(sout.shape, bf16),
            pltpu.VMEM(tqkv.shape, bf16),
            pltpu.VMEM(tout.shape, bf16),
            pltpu.VMEM((8, 6 * width), f32),
            pltpu.VMEM((width, LANES), bf16),
            pltpu.VMEM((2 * LANES, width), bf16),
            pltpu.VMEM((rows, rows), bf16),
            pltpu.VMEM((rows, width), bf16),
            pltpu.VMEM((rows, width), bf16),
            pltpu.VMEM((rows, width), bf16),
            exchange,
            exchange,
            pltpu.VMEM((peers, 1, LANES), f32),
            pltpu.VMEM((peers, 1, LANES), f32),
            pltpu.SemaphoreType.DMA((12,)),
            sems,
            sems,
            sems,
            sems,
        ],
        compiler_params=pltpu.CompilerParams(
            collective_id=0, has_side_effects=True, vmem_limit_bytes=60 * 1024 * 1024
        ),
    )(hidden, now, following, step, tags, levels, final, time_w, sqkv, sout, tqkv, tout)


def solution(mesh):
    split = P(("inner", "outer"), None)
    split3 = P(("inner", "outer"), None, None)
    sizes = (mesh.shape["inner"], mesh.shape["outer"])
    return jax.shard_map(
        functools.partial(shards, sizes),
        mesh=mesh,
        in_specs=(split, split3, split3, P(), P(("inner", "outer")))
        + (P(),) * 7,
        out_specs=(split, split3),
        check_vma=False,
    )
```

```python
import functools
import math

import jax
import jax.numpy as jnp
from jax import lax
from jax.experimental import pallas as pl
from jax.experimental.pallas import tpu as pltpu
from jax.sharding import PartitionSpec as P

HEADS = 16
STEPS = 10
LANES = 128
WINDOW = 256
GROUP = 8
norm_eps = 1e-06
f32 = jnp.float32
bf16 = jnp.bfloat16
MESH = pl.DeviceIdType.MESH


def layer_norm(values):
    average = jnp.mean(values, -1, keepdims=True)
    centred = values - average
    variance = jnp.mean(centred * centred, -1, keepdims=True)
    return centred * lax.rsqrt(variance + norm_eps)


def split_pair(values):
    high = values.astype(bf16)
    return high, (values - high.astype(f32)).astype(bf16)


def dot(a, b):
    return jnp.dot(a, b, preferred_element_type=f32)


def dot_t(a, b):
    return lax.dot_general(a, b, (((1,), (1,)), ((), ())), preferred_element_type=f32)


def kernel(
    sizes,
    hidden_hbm,
    now_hbm,
    next_hbm,
    step_hbm,
    tag_hbm,
    level_hbm,
    final_hbm,
    time_hbm,
    sqkv_hbm,
    sout_hbm,
    tqkv_hbm,
    tout_hbm,
    logp_ref,
    mean_ref,
    step_ref,
    tag_ref,
    level_ref,
    hidden_ref,
    now_ref,
    next_ref,
    final_ref,
    time_w,
    sqkv_w,
    sout_w,
    tqkv_w,
    tout_w,
    table,
    group_ref,
    spread_ref,
    mask_ref,
    k_ref,
    v_ref,
    out_buf,
    in_buf,
    back_buf,
    ret_buf,
    w_sem,
    send_sem,
    recv_sem,
    send2_sem,
    recv2_sem,
):
    inner_size, outer_size = sizes
    peers = inner_size * outer_size
    rows, width = hidden_hbm.shape
    chunks, _, count, _ = out_buf.shape
    size = rows // chunks
    head = width // HEADS
    channels = final_hbm.shape[0]
    tiles = width // LANES
    inner = lax.axis_index("inner")
    outer = lax.axis_index("outer")
    me = inner * outer_size + outer

    far = outer_size // 2 if outer_size % 2 == 0 else 0

    def outer_of(j):
        span = outer_size - far
        side = outer // span
        crossing = (1 - side) * far + lax.rem(outer + j, span)
        same = side * span + lax.rem(outer + j - far, span)
        return jnp.where(j < far, crossing, same)

    def fetch(source, target, index, lo, hi):
        return pltpu.make_async_copy(
            source.at[:, lo:hi], target.at[:, lo:hi], w_sem.at[index]
        )

    loads = [
        fetch(time_hbm, time_w, 0, 0, 2 * width),
        fetch(sqkv_hbm, sqkv_w, 1, width, 2 * width),
        fetch(sqkv_hbm, sqkv_w, 2, 2 * width, 3 * width),
        fetch(sqkv_hbm, sqkv_w, 3, 0, width),
        fetch(time_hbm, time_w, 4, 2 * width, 6 * width),
        fetch(sout_hbm, sout_w, 5, 0, width),
        fetch(tqkv_hbm, tqkv_w, 6, 0, 3 * width),
        fetch(tout_hbm, tout_w, 7, 0, width),
    ]
    rest = [
        pltpu.make_async_copy(now_hbm, now_ref, w_sem.at[9]),
        pltpu.make_async_copy(next_hbm, next_ref, w_sem.at[10]),
        pltpu.make_async_copy(final_hbm, final_ref, w_sem.at[11]),
        pltpu.make_async_copy(tag_hbm, tag_ref, w_sem.at[12]),
        pltpu.make_async_copy(level_hbm, level_ref, w_sem.at[13]),
    ]
    hidden_load = pltpu.make_async_copy(hidden_hbm, hidden_ref, w_sem.at[8])
    step_load = pltpu.make_async_copy(step_hbm, step_ref, w_sem.at[14])
    step_load.start()
    loads[0].start()
    hidden_load.start()
    for load in loads[1:6]:
        load.start()

    barrier = pltpu.get_barrier_semaphore()

    @pl.loop(1, peers)
    def _(k):
        peer = lax.rem(me + k, peers)
        pl.semaphore_signal(
            barrier,
            inc=1,
            device_id=(peer // outer_size, lax.rem(peer, outer_size)),
            device_id_type=MESH,
        )

    feature = lax.broadcasted_iota(jnp.int32, (width, LANES), 0)
    column = lax.broadcasted_iota(jnp.int32, (width, LANES), 1) * head
    group_ref[...] = jnp.where(
        (feature >= column) & (feature < column + head), 1.0, 0.0
    ).astype(bf16)
    feature = lax.broadcasted_iota(jnp.int32, (LANES, width), 1)
    column = lax.broadcasted_iota(jnp.int32, (LANES, width), 0) * head
    spread = jnp.where((feature >= column) & (feature < column + head), 1.0, 0.0).astype(bf16)
    spread_ref[0:LANES, :] = spread
    spread_ref[LANES:, :] = spread

    step_load.wait()
    time_value = jnp.full((8, LANES), step_ref[0].astype(f32)) / STEPS
    lane = lax.broadcasted_iota(jnp.int32, (8, LANES), 1).astype(f32)
    angles = 1000.0 * time_value * jnp.exp(-math.log(10000.0) * lane / LANES)
    embedded = jnp.concatenate([jnp.cos(angles), jnp.sin(angles)], 1)
    activated = (embedded / (1.0 + jnp.exp(-embedded))).astype(bf16)
    loads[0].wait()
    table[:, 0 : 2 * width] = dot(activated, time_w[:, 0 : 2 * width])

    def entry(index):
        return table[0:1, index * width : (index + 1) * width]

    hidden_load.wait()
    hidden = hidden_ref[...].astype(f32)
    normed = (layer_norm(hidden) * (1.0 + entry(1)) + entry(0)).astype(bf16)

    def head_norm(values, factor):
        total = dot((values * values).astype(bf16), group_ref[...])
        inverse = lax.rsqrt(total / head + norm_eps) * factor
        high, low = split_pair(inverse)
        return (values * dot(jnp.concatenate([high, low], 1), spread_ref[...])).astype(bf16)

    lane_id = lax.broadcasted_iota(jnp.int32, (1, WINDOW), 1)

    def own_lanes(index, tile):
        inside = (lane_id >= index * head - tile * LANES) & (
            lane_id < (index + 1) * head - tile * LANES
        )
        return jnp.where(inside, 1.0, 0.0).astype(bf16)

    def window_of(index):
        tile = min(index * head // LANES, (width - WINDOW) // LANES)
        return tile, slice(tile * LANES, tile * LANES + WINDOW)

    def attend_spatial(queries):
        tops, bottoms = [None] * tiles, [None] * tiles
        for first in range(0, HEADS, GROUP):
            group = range(first, first + GROUP)
            scores = []
            for index in group:
                tile, window = window_of(index)
                own = own_lanes(index, tile)
                scores.append(dot_t(queries[:, window] * own, k_ref[:, window]))
            weights = [jnp.exp(score).astype(bf16) for score in scores]
            for index, weight in zip(group, weights):
                tile, window = window_of(index)
                own = own_lanes(index, tile)
                mixed = dot(weight, v_ref[:, window] * own + (1.0 - own))
                for side in range(WINDOW // LANES):
                    begin = index * head - (tile + side) * LANES
                    if begin >= LANES or begin + head <= 0:
                        continue
                    top = mixed[:, side * LANES : (side + 1) * LANES]
                    bottom = mixed[:, (1 - side) * LANES : (2 - side) * LANES]
                    here = tile + side
                    if tops[here] is None:
                        tops[here], bottoms[here] = top, bottom
                    else:
                        short = lane_id[:, :LANES] >= begin
                        tops[here] = jnp.where(short, top, tops[here])
                        bottoms[here] = jnp.where(short, bottom, bottoms[here])
        return jnp.concatenate(
            [(top / bottom).astype(bf16) for top, bottom in zip(tops, bottoms)], 1
        )

    def attend_temporal(queries, keys, values):
        tops, bottoms = [None] * tiles, [None] * tiles

        def add(parts, here, part):
            parts[here] = part if parts[here] is None else parts[here] + part

        for index in range(0, HEADS, 2):
            tile, window = window_of(index)
            pair = [own_lanes(index, tile), own_lanes(index + 1, tile)]
            key = keys[:, window]
            score = dot_t(queries[:, window], jnp.concatenate([key * own for own in pair], 0))
            weight = jnp.exp(score).astype(bf16) * mask_ref[...]
            value = values[:, window]
            top = dot(weight, jnp.concatenate([value * own for own in pair], 0))
            ones = [jnp.broadcast_to(own, (size, WINDOW)) for own in pair]
            bottom = dot(weight, jnp.concatenate(ones, 0))
            for side in range(WINDOW // LANES):
                lanes = slice(side * LANES, (side + 1) * LANES)
                add(tops, tile + side, top[:, lanes])
                add(bottoms, tile + side, bottom[:, lanes])
        return jnp.concatenate(
            [(top / bottom).astype(bf16) for top, bottom in zip(tops, bottoms)], 1
        )

    loads[1].wait()
    k_ref[...] = head_norm(dot(normed, sqkv_w[:, width : 2 * width]), 1.0)
    loads[2].wait()
    v_ref[...] = dot(normed, sqkv_w[:, 2 * width : 3 * width]).astype(bf16)
    loads[3].wait()
    loads[6].start()
    loads[7].start()
    for load in rest:
        load.start()
    loads[4].wait()
    table[:, 2 * width :] = dot(activated, time_w[:, 2 * width :])
    loads[5].wait()

    def forward(chunk, inner_id, outer_id):
        return pltpu.make_async_remote_copy(
            src_ref=out_buf.at[chunk, inner_id * outer_size + outer_id],
            dst_ref=in_buf.at[chunk, me],
            send_sem=send_sem.at[chunk],
            recv_sem=recv_sem.at[chunk],
            device_id=(inner_id, outer_id),
            device_id_type=MESH,
        )

    def backward(chunk, inner_id, outer_id):
        return pltpu.make_async_remote_copy(
            src_ref=back_buf.at[chunk, inner_id * outer_size + outer_id],
            dst_ref=ret_buf.at[chunk, me],
            send_sem=send2_sem.at[chunk],
            recv_sem=recv2_sem.at[chunk],
            device_id=(inner_id, outer_id),
            device_id_type=MESH,
        )

    def everyone(chunk, source, target, sends, receives):
        return pltpu.make_async_remote_copy(
            src_ref=source.at[chunk, pl.ds(0, peers - 1)],
            dst_ref=target.at[chunk, pl.ds(0, peers - 1)],
            send_sem=sends.at[chunk],
            recv_sem=receives.at[chunk],
            device_id=(inner, outer),
            device_id_type=MESH,
        )

    own_turn = far * inner_size

    def exchange(copy, chunk):
        def send(k):
            to_inner = lax.rem(inner + lax.rem(k, inner_size), inner_size)
            copy(chunk, to_inner, outer_of(k // inner_size)).start()

        @pl.loop(0, own_turn)
        def _(k):
            send(k)

        @pl.loop(own_turn + 1, peers)
        def _(k):
            send(k)

    for chunk in range(chunks):
        lo = chunk * size
        queries = head_norm(dot(normed[lo : lo + size], sqkv_w[:, 0:width]), head**-0.5)
        attended = attend_spatial(queries)
        projected = dot(attended, sout_w[...])
        after = hidden_ref[lo : lo + size, :].astype(f32) + entry(2) * projected
        out_buf[chunk] = after.reshape(peers, count, width).astype(bf16)
        if chunk == 0:
            pl.semaphore_wait(barrier, peers - 1)
        exchange(forward, chunk)
        in_buf[chunk, me] = out_buf[chunk, me]

    place = lax.rem(lax.broadcasted_iota(jnp.int32, (size, 2 * size), 0), count)
    other = lax.rem(lax.broadcasted_iota(jnp.int32, (size, 2 * size), 1), count)
    mask_ref[...] = jnp.where(place == other, 1.0, 0.0).astype(bf16)
    slot = lax.rem(lax.broadcasted_iota(jnp.int32, (size, LANES), 0), count)
    own_slot = slot == lax.broadcasted_iota(jnp.int32, (size, LANES), 1) // channels
    loads[6].wait()
    loads[7].wait()
    for load in rest:
        load.wait()
    repeated = jnp.concatenate([final_ref[...]] * (LANES // channels), 0)

    for chunk in range(chunks):
        everyone(chunk, out_buf, in_buf, send_sem, recv_sem).wait_recv()
        after = in_buf[chunk].astype(f32).reshape(size, width)
        normed = (layer_norm(after) * (1.0 + entry(4)) + entry(3)).astype(bf16)
        queries = head_norm(dot(normed, tqkv_w[:, 0:width]), head**-0.5)
        keys = head_norm(dot(normed, tqkv_w[:, width : 2 * width]), 1.0)
        values = dot(normed, tqkv_w[:, 2 * width :]).astype(bf16)
        attended = attend_temporal(queries, keys, values)
        term = dot(attended, tout_w[...]).astype(bf16).astype(f32)
        after = in_buf[chunk].astype(f32).reshape(size, width)
        final_normed = layer_norm(after + entry(5) * term).astype(bf16)
        mixed = jnp.where(own_slot, dot_t(final_normed, repeated), 0.0)
        packed = jnp.sum(mixed.reshape(peers, count, LANES), 1)
        back_buf[chunk] = packed.reshape(peers, 1, LANES)
        exchange(backward, chunk)
        ret_buf[chunk, me] = back_buf[chunk, me]

    level = jnp.float32(0.0)
    for version in range(level_ref.shape[0]):
        level = level + jnp.where(tag_ref[0] == version, level_ref[version], 0.0)
    time_row = jnp.full((1, rows), step_ref[0].astype(f32)) / STEPS
    noise_scale = level * jnp.sqrt(time_row / (1.0 - time_row))
    factor = noise_scale * noise_scale / (2.0 * time_row)
    deviation = noise_scale * math.sqrt(1.0 / STEPS)
    lane = lax.broadcasted_iota(jnp.int32, (channels, LANES), 1)
    pick = lax.rem(lane, channels) == lax.broadcasted_iota(jnp.int32, (channels, LANES), 0)
    pick = jnp.where(pick, 1.0, 0.0).astype(bf16)
    for chunk in range(chunks):
        everyone(chunk, out_buf, in_buf, send_sem, recv_sem).wait_send()

    velocity = []
    for chunk in range(chunks):
        everyone(chunk, back_buf, ret_buf, send2_sem, recv2_sem).wait_recv()
        packed = jnp.broadcast_to(ret_buf[chunk], (peers, count, LANES)).reshape(size, LANES)
        packed = jnp.where(own_slot, packed, 0.0)
        high = packed.astype(bf16)
        residue = packed - high.astype(f32)
        middle = residue.astype(bf16)
        low = (residue - middle.astype(f32)).astype(bf16)
        velocity.append(dot_t(pick, high) + dot_t(pick, middle) + dot_t(pick, low))
    velocity = jnp.concatenate(velocity, 1)
    now = now_ref[0]
    drift = velocity + factor * (now + (1.0 - time_row) * velocity)
    next_mean = now - drift / STEPS
    mean_ref[0] = next_mean
    standard = (next_ref[0] - next_mean) / deviation
    logp_ref[...] = (
        -0.5 * jnp.mean(standard * standard, 0, keepdims=True)
        - jnp.log(deviation)
        - 0.5 * math.log(2.0 * math.pi)
    )
    for chunk in range(chunks):
        everyone(chunk, back_buf, ret_buf, send2_sem, recv2_sem).wait_send()


def shards(sizes, hidden, now, following, step, tags, levels, time_w, sqkv, sout, tqkv, tout, final):
    peers = sizes[0] * sizes[1]
    rows, width = hidden.shape
    count = rows // peers
    chunks = 2 if count % 2 == 0 else 1
    size = rows // chunks
    vmem = pl.BlockSpec(memory_space=pltpu.VMEM)
    hbm = pl.BlockSpec(memory_space=pl.ANY)
    exchange = pltpu.VMEM((chunks, peers, count // chunks, width), bf16)
    returned = pltpu.VMEM((chunks, peers, 1, LANES), f32)
    sems = pltpu.SemaphoreType.DMA((chunks,))
    return pl.pallas_call(
        functools.partial(kernel, sizes),
        out_shape=(pltpu.VMEM((1, rows), f32), pltpu.VMEM(now.shape, f32)),
        in_specs=[hbm] * 12,
        out_specs=(vmem, vmem),
        scratch_shapes=[
            pltpu.SMEM(step.shape, step.dtype),
            pltpu.SMEM(tags.shape, tags.dtype),
            pltpu.SMEM(levels.shape, levels.dtype),
            pltpu.VMEM(hidden.shape, bf16),
            pltpu.VMEM(now.shape, f32),
            pltpu.VMEM(following.shape, f32),
            pltpu.VMEM(final.shape, bf16),
            pltpu.VMEM(time_w.shape, bf16),
            pltpu.VMEM(sqkv.shape, bf16),
            pltpu.VMEM(sout.shape, bf16),
            pltpu.VMEM(tqkv.shape, bf16),
            pltpu.VMEM(tout.shape, bf16),
            pltpu.VMEM((8, 6 * width), f32),
            pltpu.VMEM((width, LANES), bf16),
            pltpu.VMEM((2 * LANES, width), bf16),
            pltpu.VMEM((size, 2 * size), bf16),
            pltpu.VMEM((rows, width), bf16),
            pltpu.VMEM((rows, width), bf16),
            exchange,
            exchange,
            returned,
            returned,
            pltpu.SemaphoreType.DMA((15,)),
            sems,
            sems,
            sems,
            sems,
        ],
        compiler_params=pltpu.CompilerParams(
            collective_id=0, has_side_effects=True, vmem_limit_bytes=60 * 1024 * 1024
        ),
    )(hidden, now, following, step, tags, levels, final, time_w, sqkv, sout, tqkv, tout)


def solution(mesh):
    split = P(("inner", "outer"), None)
    split3 = P(("inner", "outer"), None, None)
    sizes = (mesh.shape["inner"], mesh.shape["outer"])
    return jax.shard_map(
        functools.partial(shards, sizes),
        mesh=mesh,
        in_specs=(split, split3, split3, P(), P(("inner", "outer")))
        + (P(),) * 7,
        out_specs=(split, split3),
        check_vma=False,
    )
```

```python
import functools
import math

import jax
import jax.numpy as jnp
from jax import lax
from jax.experimental import pallas as pl
from jax.experimental.pallas import tpu as pltpu
from jax.sharding import PartitionSpec as P

HEADS = 16
STEPS = 10
LANES = 128
WINDOW = 256
GROUP = 8
norm_eps = 1e-06
f32 = jnp.float32
bf16 = jnp.bfloat16
MESH = pl.DeviceIdType.MESH


def layer_norm(values):
    average = jnp.mean(values, -1, keepdims=True)
    centred = values - average
    variance = jnp.mean(centred * centred, -1, keepdims=True)
    return centred * lax.rsqrt(variance + norm_eps)


def split_pair(values):
    high = values.astype(bf16)
    return high, (values - high.astype(f32)).astype(bf16)


def dot(a, b):
    return jnp.dot(a, b, preferred_element_type=f32)


def dot_t(a, b):
    return lax.dot_general(a, b, (((1,), (1,)), ((), ())), preferred_element_type=f32)


def kernel(
    sizes,
    hidden_hbm,
    now_hbm,
    next_hbm,
    step_hbm,
    tag_hbm,
    level_hbm,
    final_hbm,
    time_hbm,
    sqkv_hbm,
    sout_hbm,
    tqkv_hbm,
    tout_hbm,
    logp_ref,
    mean_ref,
    step_ref,
    tag_ref,
    level_ref,
    hidden_ref,
    now_ref,
    next_ref,
    final_ref,
    time_w,
    sqkv_w,
    sout_w,
    tqkv_w,
    tout_w,
    table,
    group_ref,
    spread_ref,
    mask_ref,
    after_ref,
    q_ref,
    k_ref,
    v_ref,
    out_buf,
    in_buf,
    back_buf,
    ret_buf,
    w_sem,
    send_sem,
    recv_sem,
    send2_sem,
    recv2_sem,
):
    inner_size, outer_size = sizes
    peers = inner_size * outer_size
    rows, width = hidden_hbm.shape
    count = rows // peers
    chunks = 2 if inner_size % 2 == 0 else 1
    halves = 2 if outer_size % 2 == 0 else 1
    span = outer_size // halves
    block_peers = peers // halves
    size = rows // chunks
    part = rows // halves
    each = inner_size // chunks
    head = width // HEADS
    channels = final_hbm.shape[0]
    tiles = width // LANES
    inner = lax.axis_index("inner")
    outer = lax.axis_index("outer")
    me = inner * outer_size + outer
    core = lax.rem(inner, chunks)

    side = outer // span

    def slot_of(inner_id, outer_id):
        return outer_id * inner_size + inner_id

    def block_of(inner_id, outer_id):
        return (lax.rem(inner_id, chunks) * outer_size + outer_id) * each + inner_id // chunks

    my_slot = slot_of(inner, outer)
    my_block = block_of(inner, outer)

    early = -(-tiles // 2) * LANES

    def fetch(source, target, index, lo, hi):
        return pltpu.make_async_copy(
            source.at[:, lo:hi], target.at[:, lo:hi], w_sem.at[index]
        )

    loads = [
        fetch(time_hbm, time_w, 0, 0, 2 * width),
        fetch(sqkv_hbm, sqkv_w, 1, width, width + early),
        fetch(sqkv_hbm, sqkv_w, 2, 2 * width, 3 * width),
        fetch(sqkv_hbm, sqkv_w, 3, 0, width),
        fetch(time_hbm, time_w, 4, 2 * width, 3 * width),
        fetch(sout_hbm, sout_w, 5, 0, width),
        fetch(tqkv_hbm, tqkv_w, 6, 0, 3 * width),
        fetch(tout_hbm, tout_w, 7, 0, width),
        fetch(sqkv_hbm, sqkv_w, 15, width + early, 2 * width),
        fetch(time_hbm, time_w, 16, 3 * width, 6 * width),
    ]
    rest = [
        pltpu.make_async_copy(now_hbm, now_ref, w_sem.at[9]),
        pltpu.make_async_copy(next_hbm, next_ref, w_sem.at[10]),
        pltpu.make_async_copy(final_hbm, final_ref, w_sem.at[11]),
        pltpu.make_async_copy(tag_hbm, tag_ref, w_sem.at[12]),
        pltpu.make_async_copy(level_hbm, level_ref, w_sem.at[13]),
    ]
    hidden_load = pltpu.make_async_copy(hidden_hbm, hidden_ref, w_sem.at[8])
    step_load = pltpu.make_async_copy(step_hbm, step_ref, w_sem.at[14])
    step_load.start()
    hidden_load.start()
    loads[0].start()
    for index in (1, 8, 2, 3, 5, 4, 6, 7, 9):
        loads[index].start()
    for load in rest:
        load.start()

    barrier = pltpu.get_barrier_semaphore()

    def wrap(value, bound):
        return jnp.where(value >= bound, value - bound, value)

    for turn in range(outer_size):
        to_outer = wrap(outer + turn, outer_size)

        @pl.loop(1 if turn == 0 else 0, inner_size)
        def _(k):
            pl.semaphore_signal(
                barrier,
                inc=1,
                device_id=(wrap(inner + k, inner_size), to_outer),
                device_id_type=MESH,
            )

    feature = lax.broadcasted_iota(jnp.int32, (width, LANES), 0)
    column = lax.broadcasted_iota(jnp.int32, (width, LANES), 1) * head
    group_ref[...] = jnp.where(
        (feature >= column) & (feature < column + head), 1.0, 0.0
    ).astype(bf16)
    feature = lax.broadcasted_iota(jnp.int32, (LANES, width), 1)
    column = lax.broadcasted_iota(jnp.int32, (LANES, width), 0) * head
    spread = jnp.where((feature >= column) & (feature < column + head), 1.0, 0.0).astype(bf16)
    spread_ref[0:LANES, :] = spread
    spread_ref[LANES:, :] = spread

    step_load.wait()
    time_value = jnp.full((8, LANES), step_ref[0].astype(f32)) / STEPS
    lane = lax.broadcasted_iota(jnp.int32, (8, LANES), 1).astype(f32)
    angles = 1000.0 * time_value * jnp.exp(-math.log(10000.0) * lane / LANES)
    embedded = jnp.concatenate([jnp.cos(angles), jnp.sin(angles)], 1)
    activated = (embedded / (1.0 + jnp.exp(-embedded))).astype(bf16)
    hidden_load.wait()
    standard = layer_norm(hidden_ref[...].astype(f32))
    loads[0].wait()
    table[:, 0 : 2 * width] = dot(activated, time_w[:, 0 : 2 * width])

    def entry(index):
        return table[0:1, index * width : (index + 1) * width]

    normed = (standard * (1.0 + entry(1)) + entry(0)).astype(bf16)

    def head_norm(values, factor):
        total = dot((values * values).astype(bf16), group_ref[...])
        inverse = lax.rsqrt(total / head + norm_eps) * factor
        high, low = split_pair(inverse)
        return (values * dot(jnp.concatenate([high, low], 1), spread_ref[...])).astype(bf16)

    lane_id = lax.broadcasted_iota(jnp.int32, (1, WINDOW), 1)

    def own_lanes(index, tile):
        inside = (lane_id >= index * head - tile * LANES) & (
            lane_id < (index + 1) * head - tile * LANES
        )
        return jnp.where(inside, 1.0, 0.0).astype(bf16)

    def window_of(index):
        tile = min(index * head // LANES, (width - WINDOW) // LANES)
        return tile, slice(tile * LANES, tile * LANES + WINDOW)

    def attend(queries, masked):
        tops, bottoms = [None] * tiles, [None] * tiles
        for first in range(0, HEADS, GROUP):
            group = range(first, first + GROUP)
            scores = []
            for index in group:
                tile, window = window_of(index)
                own = own_lanes(index, tile)
                scores.append(dot_t(queries[:, window] * own, k_ref[:, window]))
            weights = [jnp.exp(score).astype(bf16) for score in scores]
            if masked:
                weights = [weight * mask_ref[...] for weight in weights]
            for index, weight in zip(group, weights):
                tile, window = window_of(index)
                own = own_lanes(index, tile)
                mixed = dot(weight, v_ref[:, window] * own + (1.0 - own))
                for side in range(WINDOW // LANES):
                    begin = index * head - (tile + side) * LANES
                    if begin >= LANES or begin + head <= 0:
                        continue
                    top = mixed[:, side * LANES : (side + 1) * LANES]
                    bottom = mixed[:, (1 - side) * LANES : (2 - side) * LANES]
                    here = tile + side
                    if tops[here] is None:
                        tops[here], bottoms[here] = top, bottom
                    else:
                        short = lane_id[:, :LANES] >= begin
                        tops[here] = jnp.where(short, top, tops[here])
                        bottoms[here] = jnp.where(short, bottom, bottoms[here])
        return jnp.concatenate(
            [(top / bottom).astype(bf16) for top, bottom in zip(tops, bottoms)], 1
        )

    loads[1].wait()
    first = dot(normed, sqkv_w[:, width : width + early])
    loads[8].wait()
    second = dot(normed, sqkv_w[:, width + early : 2 * width])
    k_ref[...] = head_norm(jnp.concatenate([first, second], 1), 1.0)
    loads[2].wait()
    v_ref[...] = dot(normed, sqkv_w[:, 2 * width : 3 * width]).astype(bf16)
    loads[3].wait()

    def forward(inner_id, outer_id, chunk, turn):
        return pltpu.make_async_remote_copy(
            src_ref=out_buf.at[block_of(inner_id, outer_id)],
            dst_ref=in_buf.at[my_slot],
            send_sem=send_sem.at[chunk, turn],
            recv_sem=recv_sem.at[turn],
            device_id=(inner_id, outer_id),
            device_id_type=MESH,
        )

    def backward(inner_id, outer_id, turn):
        return pltpu.make_async_remote_copy(
            src_ref=back_buf.at[slot_of(inner_id, outer_id)],
            dst_ref=ret_buf.at[my_block],
            send_sem=send2_sem.at[turn],
            recv_sem=recv2_sem.at[turn],
            device_id=(inner_id, outer_id),
            device_id_type=MESH,
        )

    def partners(turn):
        return block_peers - (1 if turn == halves - 1 else 0)

    def several(source, target, sends, receives, blocks):
        return pltpu.make_async_remote_copy(
            src_ref=source.at[pl.ds(0, blocks)],
            dst_ref=target.at[pl.ds(0, blocks)],
            send_sem=sends,
            recv_sem=receives,
            device_id=(inner, outer),
            device_id_type=MESH,
        )

    def half_of(turn):
        return lax.rem(side + 1 + turn, halves)

    place = outer - side * span

    def send(chunk, turn):
        for step in range(span):
            to_outer = half_of(turn) * span + wrap(place + step, span)

            def start(k):
                to_inner = wrap(inner // chunks + k, each) * chunks + chunk
                forward(to_inner, to_outer, chunk, turn).start()

            if turn == halves - 1 and step == 0:

                @pl.when(core != chunk)
                def _():
                    start(0)

                pl.loop(1, each)(start)
            else:
                pl.loop(0, each)(start)

    for chunk in range(chunks):
        lo = chunk * size
        queries = head_norm(dot(normed[lo : lo + size], sqkv_w[:, 0:width]), head**-0.5)
        attended = attend(queries, False)
        if chunk == 0:
            loads[5].wait()
            loads[4].wait()
            table[:, 2 * width : 3 * width] = dot(activated, time_w[:, 2 * width : 3 * width])
        projected = dot(attended, sout_w[...])
        after = hidden_ref[lo : lo + size, :].astype(f32) + entry(2) * projected
        out_buf[chunk * outer_size * each : (chunk + 1) * outer_size * each] = after.reshape(
            outer_size * each, count, width
        ).astype(bf16)
        if chunk == 0:
            pl.semaphore_wait(barrier, peers - 1)
        for turn in range(halves) if chunk == 0 else reversed(range(halves)):
            send(chunk, turn)
    in_buf[my_slot] = out_buf[my_block]

    loads[9].wait()
    table[:, 3 * width :] = dot(activated, time_w[:, 3 * width :])
    row = lax.rem(lax.broadcasted_iota(jnp.int32, (rows, rows), 0), count)
    other = lax.rem(lax.broadcasted_iota(jnp.int32, (rows, rows), 1), count)
    mask_ref[...] = jnp.where(row == other, 1.0, 0.0).astype(bf16)
    slot = lax.rem(lax.broadcasted_iota(jnp.int32, (rows, LANES), 0), count)
    own_slot = slot == lax.broadcasted_iota(jnp.int32, (rows, LANES), 1) // channels
    loads[6].wait()
    loads[7].wait()
    for load in rest:
        load.wait()
    repeated = jnp.concatenate([final_ref[...]] * (LANES // channels), 0)

    for turn in reversed(range(halves)):
        lo = (halves - 1 - turn) * part
        several(out_buf, in_buf, send_sem.at[0, turn], recv_sem.at[turn], partners(turn)).wait_recv()
        after = in_buf[pl.ds(half_of(turn) * block_peers, block_peers)]
        after = after.astype(f32).reshape(part, width)
        normed = (layer_norm(after) * (1.0 + entry(4)) + entry(3)).astype(bf16)
        after_ref[lo : lo + part, :] = after.astype(bf16)
        q_ref[lo : lo + part, :] = head_norm(dot(normed, tqkv_w[:, 0:width]), head**-0.5)
        k_ref[lo : lo + part, :] = head_norm(dot(normed, tqkv_w[:, width : 2 * width]), 1.0)
        v_ref[lo : lo + part, :] = dot(normed, tqkv_w[:, 2 * width :]).astype(bf16)
    attended = attend(q_ref, True)
    term = dot(attended, tout_w[...]).astype(bf16).astype(f32)
    final_normed = layer_norm(after_ref[...].astype(f32) + entry(5) * term).astype(bf16)
    mixed = jnp.where(own_slot, dot_t(final_normed, repeated), 0.0)
    packed = jnp.sum(mixed.reshape(peers, count, LANES), 1)
    packed = packed.reshape(peers, 1, LANES)
    for turn in range(halves):
        order = halves - 1 - turn
        back_buf[pl.ds(half_of(turn) * block_peers, block_peers)] = packed[
            order * block_peers : (order + 1) * block_peers
        ]
    for turn in range(halves):

        for step in range(span):
            to_outer = half_of(turn) * span + wrap(place + step, span)

            @pl.loop(1 if turn == halves - 1 and step == 0 else 0, inner_size)
            def _(k):
                backward(wrap(inner + k, inner_size), to_outer, turn).start()

    ret_buf[my_block] = back_buf[my_slot]

    level = jnp.float32(0.0)
    for version in range(level_ref.shape[0]):
        level = level + jnp.where(tag_ref[0] == version, level_ref[version], 0.0)
    time_row = jnp.full((1, rows), step_ref[0].astype(f32)) / STEPS
    noise_scale = level * jnp.sqrt(time_row / (1.0 - time_row))
    factor = noise_scale * noise_scale / (2.0 * time_row)
    deviation = noise_scale * math.sqrt(1.0 / STEPS)
    lane = lax.broadcasted_iota(jnp.int32, (channels, LANES), 1)
    pick = lax.rem(lane, channels) == lax.broadcasted_iota(jnp.int32, (channels, LANES), 0)
    pick = jnp.where(pick, 1.0, 0.0).astype(bf16)
    for chunk in range(chunks):
        for turn in range(halves - 1):
            several(out_buf, in_buf, send_sem.at[chunk, turn], recv_sem.at[0], span * each).wait_send()
        last = halves - 1

        @pl.when(core != chunk)
        def _():
            several(out_buf, in_buf, send_sem.at[chunk, last], recv_sem.at[0], span * each).wait_send()

        @pl.when(core == chunk)
        def _():
            several(out_buf, in_buf, send_sem.at[chunk, last], recv_sem.at[0], span * each - 1).wait_send()

    for turn in range(halves):
        several(
            back_buf, ret_buf, send2_sem.at[turn], recv2_sem.at[turn], partners(turn)
        ).wait_recv()
    packed = jnp.broadcast_to(ret_buf[...], (peers, count, LANES)).reshape(rows, LANES)
    packed = jnp.where(own_slot, packed, 0.0)
    high = packed.astype(bf16)
    residue = packed - high.astype(f32)
    middle = residue.astype(bf16)
    low = (residue - middle.astype(f32)).astype(bf16)
    velocity = dot_t(pick, high) + dot_t(pick, middle) + dot_t(pick, low)
    now = now_ref[0]
    drift = velocity + factor * (now + (1.0 - time_row) * velocity)
    next_mean = now - drift / STEPS
    mean_ref[0] = next_mean
    standard = (next_ref[0] - next_mean) / deviation
    logp_ref[...] = (
        -0.5 * jnp.mean(standard * standard, 0, keepdims=True)
        - jnp.log(deviation)
        - 0.5 * math.log(2.0 * math.pi)
    )
    for turn in range(halves):
        several(
            back_buf, ret_buf, send2_sem.at[turn], recv2_sem.at[turn], partners(turn)
        ).wait_send()


def shards(sizes, hidden, now, following, step, tags, levels, time_w, sqkv, sout, tqkv, tout, final):
    peers = sizes[0] * sizes[1]
    rows, width = hidden.shape
    count = rows // peers
    vmem = pl.BlockSpec(memory_space=pltpu.VMEM)
    hbm = pl.BlockSpec(memory_space=pl.ANY)
    exchange = pltpu.VMEM((peers, count, width), bf16)
    returned = pltpu.VMEM((peers, 1, LANES), f32)
    sems = pltpu.SemaphoreType.DMA((2,))
    return pl.pallas_call(
        functools.partial(kernel, sizes),
        out_shape=(pltpu.VMEM((1, rows), f32), pltpu.VMEM(now.shape, f32)),
        in_specs=[hbm] * 12,
        out_specs=(vmem, vmem),
        scratch_shapes=[
            pltpu.SMEM(step.shape, step.dtype),
            pltpu.SMEM(tags.shape, tags.dtype),
            pltpu.SMEM(levels.shape, levels.dtype),
            pltpu.VMEM(hidden.shape, bf16),
            pltpu.VMEM(now.shape, f32),
            pltpu.VMEM(following.shape, f32),
            pltpu.VMEM(final.shape, bf16),
            pltpu.VMEM(time_w.shape, bf16),
            pltpu.VMEM(sqkv.shape, bf16),
            pltpu.VMEM(sout.shape, bf16),
            pltpu.VMEM(tqkv.shape, bf16),
            pltpu.VMEM(tout.shape, bf16),
            pltpu.VMEM((8, 6 * width), f32),
            pltpu.VMEM((width, LANES), bf16),
            pltpu.VMEM((2 * LANES, width), bf16),
            pltpu.VMEM((rows, rows), bf16),
            pltpu.VMEM((rows, width), bf16),
            pltpu.VMEM((rows, width), bf16),
            pltpu.VMEM((rows, width), bf16),
            pltpu.VMEM((rows, width), bf16),
            exchange,
            exchange,
            returned,
            returned,
            pltpu.SemaphoreType.DMA((17,)),
            pltpu.SemaphoreType.DMA((2, 2)),
            sems,
            sems,
            sems,
        ],
        compiler_params=pltpu.CompilerParams(
            collective_id=0, has_side_effects=True, vmem_limit_bytes=60 * 1024 * 1024
        ),
    )(hidden, now, following, step, tags, levels, final, time_w, sqkv, sout, tqkv, tout)


def solution(mesh):
    split = P(("inner", "outer"), None)
    split3 = P(("inner", "outer"), None, None)
    sizes = (mesh.shape["inner"], mesh.shape["outer"])
    return jax.shard_map(
        functools.partial(shards, sizes),
        mesh=mesh,
        in_specs=(split, split3, split3, P(), P(("inner", "outer")))
        + (P(),) * 7,
        out_specs=(split, split3),
        check_vma=False,
    )
```

```python
import functools
import math

import jax
import jax.numpy as jnp
from jax import lax
from jax.experimental import pallas as pl
from jax.experimental.pallas import tpu as pltpu
from jax.sharding import PartitionSpec as P

HEADS = 16
STEPS = 10
LANES = 128
WINDOW = 256
GROUP = 8
norm_eps = 1e-06
f32 = jnp.float32
bf16 = jnp.bfloat16
MESH = pl.DeviceIdType.MESH


def layer_norm(values):
    average = jnp.mean(values, -1, keepdims=True)
    centred = values - average
    variance = jnp.mean(centred * centred, -1, keepdims=True)
    return centred * lax.rsqrt(variance + norm_eps)


def split_pair(values):
    high = values.astype(bf16)
    return high, (values - high.astype(f32)).astype(bf16)


def dot(a, b):
    return jnp.dot(a, b, preferred_element_type=f32)


def dot_t(a, b):
    return lax.dot_general(a, b, (((1,), (1,)), ((), ())), preferred_element_type=f32)


def kernel(
    sizes,
    hidden_hbm,
    now_hbm,
    next_hbm,
    step_hbm,
    tag_hbm,
    level_hbm,
    final_hbm,
    time_hbm,
    sqkv_hbm,
    sout_hbm,
    tqkv_hbm,
    tout_hbm,
    logp_ref,
    mean_ref,
    step_ref,
    tag_ref,
    level_ref,
    hidden_ref,
    now_ref,
    next_ref,
    final_ref,
    time_w,
    sqkv_w,
    sout_w,
    tqkv_w,
    tout_w,
    table,
    group_ref,
    spread_ref,
    mask_ref,
    after_ref,
    q_ref,
    k_ref,
    v_ref,
    out_buf,
    in_buf,
    back_buf,
    ret_buf,
    w_sem,
    send_sem,
    recv_sem,
    send2_sem,
    recv2_sem,
):
    inner_size, outer_size = sizes
    peers = inner_size * outer_size
    rows, width = hidden_hbm.shape
    count = rows // peers
    chunks = 2 if inner_size % 2 == 0 else 1
    halves = 2 if outer_size % 2 == 0 else 1
    span = outer_size // halves
    block_peers = peers // halves
    size = rows // chunks
    part = rows // halves
    each = inner_size // chunks
    head = width // HEADS
    channels = final_hbm.shape[0]
    tiles = width // LANES
    inner = lax.axis_index("inner")
    outer = lax.axis_index("outer")
    me = inner * outer_size + outer
    core = lax.rem(inner, chunks)

    side = outer // span

    def slot_of(inner_id, outer_id):
        return outer_id * inner_size + inner_id

    def block_of(inner_id, outer_id):
        return (lax.rem(inner_id, chunks) * outer_size + outer_id) * each + inner_id // chunks

    my_slot = slot_of(inner, outer)
    my_block = block_of(inner, outer)

    early = -(-tiles // 2) * LANES

    def fetch(source, target, index, lo, hi):
        return pltpu.make_async_copy(
            source.at[:, lo:hi], target.at[:, lo:hi], w_sem.at[index]
        )

    loads = [
        fetch(time_hbm, time_w, 0, 0, 2 * width),
        fetch(sqkv_hbm, sqkv_w, 1, width, width + early),
        fetch(sqkv_hbm, sqkv_w, 2, 2 * width, 3 * width),
        fetch(sqkv_hbm, sqkv_w, 3, 0, width),
        fetch(time_hbm, time_w, 4, 2 * width, 3 * width),
        fetch(sout_hbm, sout_w, 5, 0, width),
        fetch(tqkv_hbm, tqkv_w, 6, 0, 3 * width),
        fetch(tout_hbm, tout_w, 7, 0, width),
        fetch(sqkv_hbm, sqkv_w, 15, width + early, 2 * width),
        fetch(time_hbm, time_w, 16, 3 * width, 6 * width),
    ]
    rest = [
        pltpu.make_async_copy(now_hbm, now_ref, w_sem.at[9]),
        pltpu.make_async_copy(next_hbm, next_ref, w_sem.at[10]),
        pltpu.make_async_copy(final_hbm, final_ref, w_sem.at[11]),
        pltpu.make_async_copy(tag_hbm, tag_ref, w_sem.at[12]),
        pltpu.make_async_copy(level_hbm, level_ref, w_sem.at[13]),
    ]
    hidden_load = pltpu.make_async_copy(hidden_hbm, hidden_ref, w_sem.at[8])
    step_load = pltpu.make_async_copy(step_hbm, step_ref, w_sem.at[14])
    step_load.start()
    hidden_load.start()
    loads[0].start()
    for index in (1, 8, 2, 3, 5, 4, 6, 7, 9):
        loads[index].start()
    for load in rest:
        load.start()

    barrier = pltpu.get_barrier_semaphore()

    def wrap(value, bound):
        return jnp.where(value >= bound, value - bound, value)

    for turn in range(outer_size):
        to_outer = wrap(outer + turn, outer_size)

        @pl.loop(1 if turn == 0 else 0, inner_size)
        def _(k):
            pl.semaphore_signal(
                barrier,
                inc=1,
                device_id=(wrap(inner + k, inner_size), to_outer),
                device_id_type=MESH,
            )

    feature = lax.broadcasted_iota(jnp.int32, (width, LANES), 0)
    column = lax.broadcasted_iota(jnp.int32, (width, LANES), 1) * head
    group_ref[...] = jnp.where(
        (feature >= column) & (feature < column + head), 1.0, 0.0
    ).astype(bf16)
    feature = lax.broadcasted_iota(jnp.int32, (LANES, width), 1)
    column = lax.broadcasted_iota(jnp.int32, (LANES, width), 0) * head
    spread = jnp.where((feature >= column) & (feature < column + head), 1.0, 0.0).astype(bf16)
    spread_ref[0:LANES, :] = spread
    spread_ref[LANES:, :] = spread

    step_load.wait()
    time_value = jnp.full((8, LANES), step_ref[0].astype(f32)) / STEPS
    lane = lax.broadcasted_iota(jnp.int32, (8, LANES), 1).astype(f32)
    angles = 1000.0 * time_value * jnp.exp(-math.log(10000.0) * lane / LANES)
    embedded = jnp.concatenate([jnp.cos(angles), jnp.sin(angles)], 1)
    activated = (embedded / (1.0 + jnp.exp(-embedded))).astype(bf16)
    hidden_load.wait()
    standard = layer_norm(hidden_ref[...].astype(f32))
    loads[0].wait()
    table[:, 0 : 2 * width] = dot(activated, time_w[:, 0 : 2 * width])

    def entry(index):
        return table[0:1, index * width : (index + 1) * width]

    normed = (standard * (1.0 + entry(1)) + entry(0)).astype(bf16)

    def head_norm_both(queries, keys):
        both = jnp.concatenate([queries, keys], 0)
        total = dot((both * both).astype(bf16), group_ref[...])
        inverse = lax.rsqrt(total / head + norm_eps)
        cut = queries.shape[0]
        inverse = jnp.concatenate([inverse[:cut] * head**-0.5, inverse[cut:]], 0)
        high, low = split_pair(inverse)
        both = (both * dot(jnp.concatenate([high, low], 1), spread_ref[...])).astype(bf16)
        return both[:cut], both[cut:]

    def head_norm(values, factor):
        total = dot((values * values).astype(bf16), group_ref[...])
        inverse = lax.rsqrt(total / head + norm_eps) * factor
        high, low = split_pair(inverse)
        return (values * dot(jnp.concatenate([high, low], 1), spread_ref[...])).astype(bf16)

    lane_id = lax.broadcasted_iota(jnp.int32, (1, WINDOW), 1)

    def own_lanes(index, tile):
        inside = (lane_id >= index * head - tile * LANES) & (
            lane_id < (index + 1) * head - tile * LANES
        )
        return jnp.where(inside, 1.0, 0.0).astype(bf16)

    def window_of(index):
        tile = min(index * head // LANES, (width - WINDOW) // LANES)
        return tile, slice(tile * LANES, tile * LANES + WINDOW)

    def attend(queries, masked):
        tops, bottoms = [None] * tiles, [None] * tiles
        for first in range(0, HEADS, GROUP):
            group = range(first, first + GROUP)
            scores = []
            for index in range(first, first + GROUP, 2):
                tile, window = window_of(index)
                query = queries[:, window]
                pair = [query * own_lanes(index + turn, tile) for turn in range(2)]
                score = dot_t(jnp.concatenate(pair, 0), k_ref[:, window])
                scores += [score[: query.shape[0]], score[query.shape[0] :]]
            weights = [jnp.exp(score).astype(bf16) for score in scores]
            if masked:
                weights = [weight * mask_ref[...] for weight in weights]
            for index, weight in zip(group, weights):
                tile, window = window_of(index)
                own = own_lanes(index, tile)
                mixed = dot(weight, v_ref[:, window] * own + (1.0 - own))
                for side in range(WINDOW // LANES):
                    begin = index * head - (tile + side) * LANES
                    if begin >= LANES or begin + head <= 0:
                        continue
                    top = mixed[:, side * LANES : (side + 1) * LANES]
                    bottom = mixed[:, (1 - side) * LANES : (2 - side) * LANES]
                    here = tile + side
                    if tops[here] is None:
                        tops[here], bottoms[here] = top, bottom
                    else:
                        short = lane_id[:, :LANES] >= begin
                        tops[here] = jnp.where(short, top, tops[here])
                        bottoms[here] = jnp.where(short, bottom, bottoms[here])
        return jnp.concatenate(
            [(top / bottom).astype(bf16) for top, bottom in zip(tops, bottoms)], 1
        )

    loads[1].wait()
    first = dot(normed, sqkv_w[:, width : width + early])
    loads[8].wait()
    second = dot(normed, sqkv_w[:, width + early : 2 * width])
    k_ref[...] = head_norm(jnp.concatenate([first, second], 1), 1.0)
    loads[2].wait()
    v_ref[...] = dot(normed, sqkv_w[:, 2 * width : 3 * width]).astype(bf16)
    loads[3].wait()

    def forward(inner_id, outer_id, chunk, turn):
        return pltpu.make_async_remote_copy(
            src_ref=out_buf.at[block_of(inner_id, outer_id)],
            dst_ref=in_buf.at[my_slot],
            send_sem=send_sem.at[chunk, turn],
            recv_sem=recv_sem.at[turn],
            device_id=(inner_id, outer_id),
            device_id_type=MESH,
        )

    def backward(inner_id, outer_id, turn):
        return pltpu.make_async_remote_copy(
            src_ref=back_buf.at[slot_of(inner_id, outer_id)],
            dst_ref=ret_buf.at[my_block],
            send_sem=send2_sem.at[turn],
            recv_sem=recv2_sem.at[turn],
            device_id=(inner_id, outer_id),
            device_id_type=MESH,
        )

    def partners(turn):
        return block_peers - (1 if turn == halves - 1 else 0)

    def several(source, target, sends, receives, blocks):
        return pltpu.make_async_remote_copy(
            src_ref=source.at[pl.ds(0, blocks)],
            dst_ref=target.at[pl.ds(0, blocks)],
            send_sem=sends,
            recv_sem=receives,
            device_id=(inner, outer),
            device_id_type=MESH,
        )

    def half_of(turn):
        return lax.rem(side + 1 + turn, halves)

    place = outer - side * span

    def send(chunk, turn):
        for step in range(span):
            to_outer = half_of(turn) * span + wrap(place + step, span)

            def start(k):
                to_inner = wrap(inner // chunks + k, each) * chunks + chunk
                forward(to_inner, to_outer, chunk, turn).start()

            if turn == halves - 1 and step == 0:

                @pl.when(core != chunk)
                def _():
                    start(0)

                pl.loop(1, each)(start)
            else:
                pl.loop(0, each)(start)

    for chunk in range(chunks):
        lo = chunk * size
        queries = head_norm(dot(normed[lo : lo + size], sqkv_w[:, 0:width]), head**-0.5)
        attended = attend(queries, False)
        if chunk == 0:
            loads[5].wait()
            loads[4].wait()
            table[:, 2 * width : 3 * width] = dot(activated, time_w[:, 2 * width : 3 * width])
        projected = dot(attended, sout_w[...])
        after = hidden_ref[lo : lo + size, :].astype(f32) + entry(2) * projected
        out_buf[chunk * outer_size * each : (chunk + 1) * outer_size * each] = after.reshape(
            outer_size * each, count, width
        ).astype(bf16)
        if chunk == 0:
            pl.semaphore_wait(barrier, peers - 1)
        for turn in range(halves) if chunk == 0 else reversed(range(halves)):
            send(chunk, turn)
    in_buf[my_slot] = out_buf[my_block]

    loads[9].wait()
    table[:, 3 * width :] = dot(activated, time_w[:, 3 * width :])
    row = lax.rem(lax.broadcasted_iota(jnp.int32, (rows, rows), 0), count)
    other = lax.rem(lax.broadcasted_iota(jnp.int32, (rows, rows), 1), count)
    mask_ref[...] = jnp.where(row == other, 1.0, 0.0).astype(bf16)
    slot = lax.rem(lax.broadcasted_iota(jnp.int32, (rows, LANES), 0), count)
    own_slot = slot == lax.broadcasted_iota(jnp.int32, (rows, LANES), 1) // channels
    loads[6].wait()
    loads[7].wait()
    for load in rest:
        load.wait()
    repeated = jnp.concatenate([final_ref[...]] * (LANES // channels), 0)

    for turn in reversed(range(halves)):
        lo = (halves - 1 - turn) * part
        several(out_buf, in_buf, send_sem.at[0, turn], recv_sem.at[turn], partners(turn)).wait_recv()
        after = in_buf[pl.ds(half_of(turn) * block_peers, block_peers)]
        after = after.astype(f32).reshape(part, width)
        normed = (layer_norm(after) * (1.0 + entry(4)) + entry(3)).astype(bf16)
        after_ref[lo : lo + part, :] = after.astype(bf16)
        q_ref[lo : lo + part, :], k_ref[lo : lo + part, :] = head_norm_both(
            dot(normed, tqkv_w[:, 0:width]), dot(normed, tqkv_w[:, width : 2 * width])
        )
        v_ref[lo : lo + part, :] = dot(normed, tqkv_w[:, 2 * width :]).astype(bf16)
    attended = attend(q_ref, True)
    term = dot(attended, tout_w[...]).astype(bf16).astype(f32)
    final_normed = layer_norm(after_ref[...].astype(f32) + entry(5) * term).astype(bf16)
    mixed = jnp.where(own_slot, dot_t(final_normed, repeated), 0.0)
    packed = jnp.sum(mixed.reshape(peers, count, LANES), 1)
    packed = packed.reshape(peers, 1, LANES)
    for turn in range(halves):
        order = halves - 1 - turn
        back_buf[pl.ds(half_of(turn) * block_peers, block_peers)] = packed[
            order * block_peers : (order + 1) * block_peers
        ]
    for turn in range(halves):

        for step in range(span):
            to_outer = half_of(turn) * span + wrap(place + step, span)

            @pl.loop(1 if turn == halves - 1 and step == 0 else 0, inner_size)
            def _(k):
                backward(wrap(inner + k, inner_size), to_outer, turn).start()

    ret_buf[my_block] = back_buf[my_slot]

    level = jnp.float32(0.0)
    for version in range(level_ref.shape[0]):
        level = level + jnp.where(tag_ref[0] == version, level_ref[version], 0.0)
    time_row = jnp.full((1, rows), step_ref[0].astype(f32)) / STEPS
    noise_scale = level * jnp.sqrt(time_row / (1.0 - time_row))
    factor = noise_scale * noise_scale / (2.0 * time_row)
    deviation = noise_scale * math.sqrt(1.0 / STEPS)
    lane = lax.broadcasted_iota(jnp.int32, (channels, LANES), 1)
    pick = lax.rem(lane, channels) == lax.broadcasted_iota(jnp.int32, (channels, LANES), 0)
    pick = jnp.where(pick, 1.0, 0.0).astype(bf16)
    for chunk in range(chunks):
        for turn in range(halves - 1):
            several(out_buf, in_buf, send_sem.at[chunk, turn], recv_sem.at[0], span * each).wait_send()
        last = halves - 1

        @pl.when(core != chunk)
        def _():
            several(out_buf, in_buf, send_sem.at[chunk, last], recv_sem.at[0], span * each).wait_send()

        @pl.when(core == chunk)
        def _():
            several(out_buf, in_buf, send_sem.at[chunk, last], recv_sem.at[0], span * each - 1).wait_send()

    for turn in range(halves):
        several(
            back_buf, ret_buf, send2_sem.at[turn], recv2_sem.at[turn], partners(turn)
        ).wait_recv()
    packed = jnp.broadcast_to(ret_buf[...], (peers, count, LANES)).reshape(rows, LANES)
    packed = jnp.where(own_slot, packed, 0.0)
    high = packed.astype(bf16)
    residue = packed - high.astype(f32)
    middle = residue.astype(bf16)
    low = (residue - middle.astype(f32)).astype(bf16)
    velocity = dot_t(pick, high) + dot_t(pick, middle) + dot_t(pick, low)
    now = now_ref[0]
    drift = velocity + factor * (now + (1.0 - time_row) * velocity)
    next_mean = now - drift / STEPS
    mean_ref[0] = next_mean
    standard = (next_ref[0] - next_mean) / deviation
    logp_ref[...] = (
        -0.5 * jnp.mean(standard * standard, 0, keepdims=True)
        - jnp.log(deviation)
        - 0.5 * math.log(2.0 * math.pi)
    )
    for turn in range(halves):
        several(
            back_buf, ret_buf, send2_sem.at[turn], recv2_sem.at[turn], partners(turn)
        ).wait_send()


def shards(sizes, hidden, now, following, step, tags, levels, time_w, sqkv, sout, tqkv, tout, final):
    peers = sizes[0] * sizes[1]
    rows, width = hidden.shape
    count = rows // peers
    vmem = pl.BlockSpec(memory_space=pltpu.VMEM)
    hbm = pl.BlockSpec(memory_space=pl.ANY)
    exchange = pltpu.VMEM((peers, count, width), bf16)
    returned = pltpu.VMEM((peers, 1, LANES), f32)
    sems = pltpu.SemaphoreType.DMA((2,))
    return pl.pallas_call(
        functools.partial(kernel, sizes),
        out_shape=(pltpu.VMEM((1, rows), f32), pltpu.VMEM(now.shape, f32)),
        in_specs=[hbm] * 12,
        out_specs=(vmem, vmem),
        scratch_shapes=[
            pltpu.SMEM(step.shape, step.dtype),
            pltpu.SMEM(tags.shape, tags.dtype),
            pltpu.SMEM(levels.shape, levels.dtype),
            pltpu.VMEM(hidden.shape, bf16),
            pltpu.VMEM(now.shape, f32),
            pltpu.VMEM(following.shape, f32),
            pltpu.VMEM(final.shape, bf16),
            pltpu.VMEM(time_w.shape, bf16),
            pltpu.VMEM(sqkv.shape, bf16),
            pltpu.VMEM(sout.shape, bf16),
            pltpu.VMEM(tqkv.shape, bf16),
            pltpu.VMEM(tout.shape, bf16),
            pltpu.VMEM((8, 6 * width), f32),
            pltpu.VMEM((width, LANES), bf16),
            pltpu.VMEM((2 * LANES, width), bf16),
            pltpu.VMEM((rows, rows), bf16),
            pltpu.VMEM((rows, width), bf16),
            pltpu.VMEM((rows, width), bf16),
            pltpu.VMEM((rows, width), bf16),
            pltpu.VMEM((rows, width), bf16),
            exchange,
            exchange,
            returned,
            returned,
            pltpu.SemaphoreType.DMA((17,)),
            pltpu.SemaphoreType.DMA((2, 2)),
            sems,
            sems,
            sems,
        ],
        compiler_params=pltpu.CompilerParams(
            collective_id=0, has_side_effects=True, vmem_limit_bytes=60 * 1024 * 1024
        ),
    )(hidden, now, following, step, tags, levels, final, time_w, sqkv, sout, tqkv, tout)


def solution(mesh):
    split = P(("inner", "outer"), None)
    split3 = P(("inner", "outer"), None, None)
    sizes = (mesh.shape["inner"], mesh.shape["outer"])
    return jax.shard_map(
        functools.partial(shards, sizes),
        mesh=mesh,
        in_specs=(split, split3, split3, P(), P(("inner", "outer")))
        + (P(),) * 7,
        out_specs=(split, split3),
        check_vma=False,
    )
```

```python
import functools
import math

import jax
import jax.numpy as jnp
from jax import lax
from jax.experimental import pallas as pl
from jax.experimental.pallas import tpu as pltpu
from jax.sharding import PartitionSpec as P

HEADS = 16
STEPS = 10
LANES = 128
WINDOW = 256
GROUP = 8
norm_eps = 1e-06
f32 = jnp.float32
bf16 = jnp.bfloat16
MESH = pl.DeviceIdType.MESH


def layer_norm(values):
    average = jnp.mean(values, -1, keepdims=True)
    centred = values - average
    variance = jnp.mean(centred * centred, -1, keepdims=True)
    return centred * lax.rsqrt(variance + norm_eps)


def split_pair(values):
    high = values.astype(bf16)
    return high, (values - high.astype(f32)).astype(bf16)


def dot(a, b):
    return jnp.dot(a, b, preferred_element_type=f32)


def dot_t(a, b):
    return lax.dot_general(a, b, (((1,), (1,)), ((), ())), preferred_element_type=f32)


def kernel(
    sizes,
    hidden_hbm,
    now_hbm,
    next_hbm,
    step_hbm,
    tag_hbm,
    level_hbm,
    final_hbm,
    time_hbm,
    sqkv_hbm,
    sout_hbm,
    tqkv_hbm,
    tout_hbm,
    logp_ref,
    mean_ref,
    step_ref,
    tag_ref,
    level_ref,
    hidden_ref,
    now_ref,
    next_ref,
    final_ref,
    time_w,
    sqkv_w,
    sout_w,
    tqkv_w,
    tout_w,
    table,
    group_ref,
    spread_ref,
    mask_ref,
    after_ref,
    q_ref,
    k_ref,
    v_ref,
    out_buf,
    in_buf,
    back_buf,
    ret_buf,
    w_sem,
    send_sem,
    recv_sem,
    send2_sem,
    recv2_sem,
):
    inner_size, outer_size = sizes
    peers = inner_size * outer_size
    rows, width = hidden_hbm.shape
    count = rows // peers
    chunks = 2 if inner_size % 2 == 0 else 1
    halves = 2 if outer_size % 2 == 0 else 1
    span = outer_size // halves
    block_peers = peers // halves
    size = rows // chunks
    part = rows // halves
    each = inner_size // chunks
    head = width // HEADS
    channels = final_hbm.shape[0]
    tiles = width // LANES
    inner = lax.axis_index("inner")
    outer = lax.axis_index("outer")
    me = inner * outer_size + outer
    core = lax.rem(inner, chunks)

    side = outer // span

    def slot_of(inner_id, outer_id):
        return outer_id * inner_size + inner_id

    def block_of(inner_id, outer_id):
        return (lax.rem(inner_id, chunks) * outer_size + outer_id) * each + inner_id // chunks

    my_slot = slot_of(inner, outer)
    my_block = block_of(inner, outer)

    early = -(-tiles // 2) * LANES

    def fetch(source, target, index, lo, hi):
        return pltpu.make_async_copy(
            source.at[:, lo:hi], target.at[:, lo:hi], w_sem.at[index]
        )

    loads = [
        fetch(time_hbm, time_w, 0, 0, 2 * width),
        fetch(sqkv_hbm, sqkv_w, 1, width, width + early),
        fetch(sqkv_hbm, sqkv_w, 2, 2 * width, 3 * width),
        fetch(sqkv_hbm, sqkv_w, 3, 0, width),
        fetch(time_hbm, time_w, 4, 2 * width, 3 * width),
        fetch(sout_hbm, sout_w, 5, 0, width),
        fetch(tqkv_hbm, tqkv_w, 6, 0, 3 * width),
        fetch(tout_hbm, tout_w, 7, 0, width),
        fetch(sqkv_hbm, sqkv_w, 15, width + early, 2 * width),
        fetch(time_hbm, time_w, 16, 3 * width, 6 * width),
    ]
    rest = [
        pltpu.make_async_copy(now_hbm, now_ref, w_sem.at[9]),
        pltpu.make_async_copy(next_hbm, next_ref, w_sem.at[10]),
        pltpu.make_async_copy(final_hbm, final_ref, w_sem.at[11]),
        pltpu.make_async_copy(tag_hbm, tag_ref, w_sem.at[12]),
        pltpu.make_async_copy(level_hbm, level_ref, w_sem.at[13]),
    ]
    hidden_load = pltpu.make_async_copy(hidden_hbm, hidden_ref, w_sem.at[8])
    step_load = pltpu.make_async_copy(step_hbm, step_ref, w_sem.at[14])
    step_load.start()
    hidden_load.start()
    loads[0].start()
    for index in (1, 8, 2, 3, 5, 4, 6, 7, 9):
        loads[index].start()
    for load in rest:
        load.start()

    barrier = pltpu.get_barrier_semaphore()

    def wrap(value, bound):
        return jnp.where(value >= bound, value - bound, value)

    for turn in range(outer_size):
        to_outer = wrap(outer + turn, outer_size)

        @pl.loop(1 if turn == 0 else 0, inner_size)
        def _(k):
            pl.semaphore_signal(
                barrier,
                inc=1,
                device_id=(wrap(inner + k, inner_size), to_outer),
                device_id_type=MESH,
            )

    feature = lax.broadcasted_iota(jnp.int32, (width, LANES), 0)
    column = lax.broadcasted_iota(jnp.int32, (width, LANES), 1) * head
    group_ref[...] = jnp.where(
        (feature >= column) & (feature < column + head), 1.0, 0.0
    ).astype(bf16)
    feature = lax.broadcasted_iota(jnp.int32, (LANES, width), 1)
    column = lax.broadcasted_iota(jnp.int32, (LANES, width), 0) * head
    spread = jnp.where((feature >= column) & (feature < column + head), 1.0, 0.0).astype(bf16)
    spread_ref[0:LANES, :] = spread
    spread_ref[LANES:, :] = spread

    step_load.wait()
    time_value = jnp.full((8, LANES), step_ref[0].astype(f32)) / STEPS
    lane = lax.broadcasted_iota(jnp.int32, (8, LANES), 1).astype(f32)
    angles = 1000.0 * time_value * jnp.exp(-math.log(10000.0) * lane / LANES)
    embedded = jnp.concatenate([jnp.cos(angles), jnp.sin(angles)], 1)
    activated = (embedded / (1.0 + jnp.exp(-embedded))).astype(bf16)
    hidden_load.wait()
    standard = layer_norm(hidden_ref[...].astype(f32))
    loads[0].wait()
    table[:, 0 : 2 * width] = dot(activated, time_w[:, 0 : 2 * width])

    def entry(index):
        return table[0:1, index * width : (index + 1) * width]

    normed = (standard * (1.0 + entry(1)) + entry(0)).astype(bf16)

    def head_norm_both(queries, keys):
        both = jnp.concatenate([queries, keys], 0)
        total = dot((both * both).astype(bf16), group_ref[...])
        inverse = lax.rsqrt(total / head + norm_eps)
        cut = queries.shape[0]
        inverse = jnp.concatenate([inverse[:cut] * head**-0.5, inverse[cut:]], 0)
        high, low = split_pair(inverse)
        both = (both * dot(jnp.concatenate([high, low], 1), spread_ref[...])).astype(bf16)
        return both[:cut], both[cut:]

    def head_norm(values, factor):
        total = dot((values * values).astype(bf16), group_ref[...])
        inverse = lax.rsqrt(total / head + norm_eps) * factor
        high, low = split_pair(inverse)
        return (values * dot(jnp.concatenate([high, low], 1), spread_ref[...])).astype(bf16)

    lane_id = lax.broadcasted_iota(jnp.int32, (1, WINDOW), 1)

    def own_lanes(index, tile):
        inside = (lane_id >= index * head - tile * LANES) & (
            lane_id < (index + 1) * head - tile * LANES
        )
        return jnp.where(inside, 1.0, 0.0).astype(bf16)

    def window_of(index):
        tile = min(index * head // LANES, (width - WINDOW) // LANES)
        return tile, slice(tile * LANES, tile * LANES + WINDOW)

    def attend(queries, masked):
        tops, bottoms = [None] * tiles, [None] * tiles
        for first in range(0, HEADS, GROUP):
            group = range(first, first + GROUP)
            scores = []
            for index in range(first, first + GROUP, 2):
                tile, window = window_of(index)
                query = queries[:, window]
                pair = [query * own_lanes(index + turn, tile) for turn in range(2)]
                score = dot_t(jnp.concatenate(pair, 0), k_ref[:, window])
                scores += [score[: query.shape[0]], score[query.shape[0] :]]
            weights = [jnp.exp(score).astype(bf16) for score in scores]
            if masked:
                weights = [weight * mask_ref[...] for weight in weights]
            for index, weight in zip(group, weights):
                tile, window = window_of(index)
                own = own_lanes(index, tile)
                mixed = dot(weight, jnp.where(own > 0.5, v_ref[:, window], own + 1.0))
                for side in range(WINDOW // LANES):
                    begin = index * head - (tile + side) * LANES
                    if begin >= LANES or begin + head <= 0:
                        continue
                    top = mixed[:, side * LANES : (side + 1) * LANES]
                    bottom = mixed[:, (1 - side) * LANES : (2 - side) * LANES]
                    here = tile + side
                    if tops[here] is None:
                        tops[here], bottoms[here] = top, bottom
                    else:
                        short = lane_id[:, :LANES] >= begin
                        tops[here] = jnp.where(short, top, tops[here])
                        bottoms[here] = jnp.where(short, bottom, bottoms[here])
        return jnp.concatenate(
            [(top / bottom).astype(bf16) for top, bottom in zip(tops, bottoms)], 1
        )

    loads[1].wait()
    first = dot(normed, sqkv_w[:, width : width + early])
    loads[8].wait()
    second = dot(normed, sqkv_w[:, width + early : 2 * width])
    k_ref[...] = head_norm(jnp.concatenate([first, second], 1), 1.0)
    loads[2].wait()
    v_ref[...] = dot(normed, sqkv_w[:, 2 * width : 3 * width]).astype(bf16)
    loads[3].wait()

    def forward(inner_id, outer_id, chunk, turn):
        return pltpu.make_async_remote_copy(
            src_ref=out_buf.at[block_of(inner_id, outer_id)],
            dst_ref=in_buf.at[my_slot],
            send_sem=send_sem.at[chunk, turn],
            recv_sem=recv_sem.at[outer],
            device_id=(inner_id, outer_id),
            device_id_type=MESH,
        )

    def backward(inner_id, outer_id, turn):
        return pltpu.make_async_remote_copy(
            src_ref=back_buf.at[slot_of(inner_id, outer_id)],
            dst_ref=ret_buf.at[my_block],
            send_sem=send2_sem.at[turn],
            recv_sem=recv2_sem.at[turn],
            device_id=(inner_id, outer_id),
            device_id_type=MESH,
        )

    def partners(turn):
        return block_peers - (1 if turn == halves - 1 else 0)

    def several(source, target, sends, receives, blocks):
        return pltpu.make_async_remote_copy(
            src_ref=source.at[pl.ds(0, blocks)],
            dst_ref=target.at[pl.ds(0, blocks)],
            send_sem=sends,
            recv_sem=receives,
            device_id=(inner, outer),
            device_id_type=MESH,
        )

    def half_of(turn):
        return lax.rem(side + 1 + turn, halves)

    place = outer - side * span

    def send(chunk, turn):
        for step in range(span):
            to_outer = half_of(turn) * span + wrap(place + step, span)

            def start(k):
                to_inner = wrap(inner // chunks + k, each) * chunks + chunk
                forward(to_inner, to_outer, chunk, turn).start()

            if turn == halves - 1 and step == 0:

                @pl.when(core != chunk)
                def _():
                    start(0)

                pl.loop(1, each)(start)
            else:
                pl.loop(0, each)(start)

    for chunk in range(chunks):
        lo = chunk * size
        queries = head_norm(dot(normed[lo : lo + size], sqkv_w[:, 0:width]), head**-0.5)
        attended = attend(queries, False)
        if chunk == 0:
            loads[5].wait()
            loads[4].wait()
            table[:, 2 * width : 3 * width] = dot(activated, time_w[:, 2 * width : 3 * width])
        projected = dot(attended, sout_w[...])
        after = hidden_ref[lo : lo + size, :].astype(f32) + entry(2) * projected
        out_buf[chunk * outer_size * each : (chunk + 1) * outer_size * each] = after.reshape(
            outer_size * each, count, width
        ).astype(bf16)
        if chunk == 0:
            pl.semaphore_wait(barrier, peers - 1)
        for turn in range(halves) if chunk == 0 else reversed(range(halves)):
            send(chunk, turn)
    in_buf[my_slot] = out_buf[my_block]

    loads[9].wait()
    table[:, 3 * width :] = dot(activated, time_w[:, 3 * width :])
    row = lax.rem(lax.broadcasted_iota(jnp.int32, (rows, rows), 0), count)
    other = lax.rem(lax.broadcasted_iota(jnp.int32, (rows, rows), 1), count)
    mask_ref[...] = jnp.where(row == other, 1.0, 0.0).astype(bf16)
    slot = lax.rem(lax.broadcasted_iota(jnp.int32, (rows, LANES), 0), count)
    own_slot = slot == lax.broadcasted_iota(jnp.int32, (rows, LANES), 1) // channels
    loads[6].wait()
    loads[7].wait()
    for load in rest:
        load.wait()
    repeated = jnp.concatenate([final_ref[...]] * (LANES // channels), 0)

    stages = [[side * span + step for step in range(span)]]
    if halves == 2:
        for step in range(span):
            stages.append([jnp.where(side == 0, outer_size - 1 - step, step)])

    def arrive(outer_id):
        def wait(blocks):
            several(
                out_buf, in_buf, send_sem.at[0, 0], recv_sem.at[outer_id], blocks
            ).wait_recv()

        pl.when(outer_id == outer)(lambda: wait(inner_size - 1))
        pl.when(outer_id != outer)(lambda: wait(inner_size))

    def enter(outer_ids, lo):
        pieces = []
        for outer_id in outer_ids:
            arrive(outer_id)
            piece = in_buf[pl.ds(outer_id * inner_size, inner_size)]
            pieces.append(piece.astype(f32).reshape(inner_size * count, width))
        after = jnp.concatenate(pieces, 0)
        hi = lo + after.shape[0]
        normed = (layer_norm(after) * (1.0 + entry(4)) + entry(3)).astype(bf16)
        after_ref[lo:hi, :] = after.astype(bf16)
        mixed = dot(normed, tqkv_w[:, 0 : 2 * width])
        q_ref[lo:hi, :], k_ref[lo:hi, :] = head_norm_both(mixed[:, :width], mixed[:, width:])
        v_ref[lo:hi, :] = dot(normed, tqkv_w[:, 2 * width :]).astype(bf16)

    enter(stages[0], 0)
    if halves == 2:
        rim = (outer == 0) | (outer == outer_size - 1)
        distant = [stage[0] for stage in stages[1:]]

        @pl.when(rim)
        def _():
            enter(distant, span * inner_size * count)

        @pl.when(jnp.logical_not(rim))
        def _():
            for step in range(span):
                enter(distant[step : step + 1], (span + step) * inner_size * count)

    attended = attend(q_ref, True)
    term = dot(attended, tout_w[...]).astype(bf16).astype(f32)
    final_normed = layer_norm(after_ref[...].astype(f32) + entry(5) * term).astype(bf16)
    mixed = jnp.where(own_slot, dot_t(final_normed, repeated), 0.0)
    packed = jnp.sum(mixed.reshape(peers, count, LANES), 1)
    packed = packed.reshape(peers, 1, LANES)
    done = 0
    for stage in stages:
        blocks = len(stage) * inner_size
        back_buf[pl.ds(stage[0] * inner_size, blocks)] = packed[done : done + blocks]
        done += blocks
    for turn in range(halves):

        for step in range(span):
            to_outer = half_of(turn) * span + wrap(place + step, span)

            @pl.loop(1 if turn == halves - 1 and step == 0 else 0, inner_size)
            def _(k):
                backward(wrap(inner + k, inner_size), to_outer, turn).start()

    ret_buf[my_block] = back_buf[my_slot]

    level = jnp.float32(0.0)
    for version in range(level_ref.shape[0]):
        level = level + jnp.where(tag_ref[0] == version, level_ref[version], 0.0)
    time_row = jnp.full((1, rows), step_ref[0].astype(f32)) / STEPS
    noise_scale = level * jnp.sqrt(time_row / (1.0 - time_row))
    factor = noise_scale * noise_scale / (2.0 * time_row)
    deviation = noise_scale * math.sqrt(1.0 / STEPS)
    lane = lax.broadcasted_iota(jnp.int32, (channels, LANES), 1)
    pick = lax.rem(lane, channels) == lax.broadcasted_iota(jnp.int32, (channels, LANES), 0)
    pick = jnp.where(pick, 1.0, 0.0).astype(bf16)
    for chunk in range(chunks):
        for turn in range(halves - 1):
            several(out_buf, in_buf, send_sem.at[chunk, turn], recv_sem.at[0], span * each).wait_send()
        last = halves - 1

        @pl.when(core != chunk)
        def _():
            several(out_buf, in_buf, send_sem.at[chunk, last], recv_sem.at[0], span * each).wait_send()

        @pl.when(core == chunk)
        def _():
            several(out_buf, in_buf, send_sem.at[chunk, last], recv_sem.at[0], span * each - 1).wait_send()

    for turn in range(halves):
        several(
            back_buf, ret_buf, send2_sem.at[turn], recv2_sem.at[turn], partners(turn)
        ).wait_recv()
    packed = jnp.broadcast_to(ret_buf[...], (peers, count, LANES)).reshape(rows, LANES)
    packed = jnp.where(own_slot, packed, 0.0)
    high = packed.astype(bf16)
    residue = packed - high.astype(f32)
    middle = residue.astype(bf16)
    low = (residue - middle.astype(f32)).astype(bf16)
    velocity = dot_t(pick, high) + dot_t(pick, middle) + dot_t(pick, low)
    now = now_ref[0]
    drift = velocity + factor * (now + (1.0 - time_row) * velocity)
    next_mean = now - drift / STEPS
    mean_ref[0] = next_mean
    standard = (next_ref[0] - next_mean) / deviation
    logp_ref[...] = (
        -0.5 * jnp.mean(standard * standard, 0, keepdims=True)
        - jnp.log(deviation)
        - 0.5 * math.log(2.0 * math.pi)
    )
    for turn in range(halves):
        several(
            back_buf, ret_buf, send2_sem.at[turn], recv2_sem.at[turn], partners(turn)
        ).wait_send()


def shards(sizes, hidden, now, following, step, tags, levels, time_w, sqkv, sout, tqkv, tout, final):
    peers = sizes[0] * sizes[1]
    rows, width = hidden.shape
    count = rows // peers
    vmem = pl.BlockSpec(memory_space=pltpu.VMEM)
    hbm = pl.BlockSpec(memory_space=pl.ANY)
    exchange = pltpu.VMEM((peers, count, width), bf16)
    returned = pltpu.VMEM((peers, 1, LANES), f32)
    sems = pltpu.SemaphoreType.DMA((2,))
    arrivals = pltpu.SemaphoreType.DMA((sizes[1],))
    return pl.pallas_call(
        functools.partial(kernel, sizes),
        out_shape=(pltpu.VMEM((1, rows), f32), pltpu.VMEM(now.shape, f32)),
        in_specs=[hbm] * 12,
        out_specs=(vmem, vmem),
        scratch_shapes=[
            pltpu.SMEM(step.shape, step.dtype),
            pltpu.SMEM(tags.shape, tags.dtype),
            pltpu.SMEM(levels.shape, levels.dtype),
            pltpu.VMEM(hidden.shape, bf16),
            pltpu.VMEM(now.shape, f32),
            pltpu.VMEM(following.shape, f32),
            pltpu.VMEM(final.shape, bf16),
            pltpu.VMEM(time_w.shape, bf16),
            pltpu.VMEM(sqkv.shape, bf16),
            pltpu.VMEM(sout.shape, bf16),
            pltpu.VMEM(tqkv.shape, bf16),
            pltpu.VMEM(tout.shape, bf16),
            pltpu.VMEM((8, 6 * width), f32),
            pltpu.VMEM((width, LANES), bf16),
            pltpu.VMEM((2 * LANES, width), bf16),
            pltpu.VMEM((rows, rows), bf16),
            pltpu.VMEM((rows, width), bf16),
            pltpu.VMEM((rows, width), bf16),
            pltpu.VMEM((rows, width), bf16),
            pltpu.VMEM((rows, width), bf16),
            exchange,
            exchange,
            returned,
            returned,
            pltpu.SemaphoreType.DMA((17,)),
            pltpu.SemaphoreType.DMA((2, 2)),
            arrivals,
            sems,
            sems,
        ],
        compiler_params=pltpu.CompilerParams(
            collective_id=0, has_side_effects=True, vmem_limit_bytes=60 * 1024 * 1024
        ),
    )(hidden, now, following, step, tags, levels, final, time_w, sqkv, sout, tqkv, tout)


def solution(mesh):
    split = P(("inner", "outer"), None)
    split3 = P(("inner", "outer"), None, None)
    sizes = (mesh.shape["inner"], mesh.shape["outer"])
    return jax.shard_map(
        functools.partial(shards, sizes),
        mesh=mesh,
        in_specs=(split, split3, split3, P(), P(("inner", "outer")))
        + (P(),) * 7,
        out_specs=(split, split3),
        check_vma=False,
    )
```

```python
import functools
import math

import jax
import jax.numpy as jnp
from jax import lax
from jax.experimental import pallas as pl
from jax.experimental.pallas import tpu as pltpu
from jax.sharding import PartitionSpec as P

HEADS = 16
STEPS = 10
LANES = 128
WINDOW = 256
GROUP = 8
norm_eps = 1e-06
f32 = jnp.float32
bf16 = jnp.bfloat16
MESH = pl.DeviceIdType.MESH


def layer_norm(values):
    average = jnp.mean(values, -1, keepdims=True)
    centred = values - average
    variance = jnp.mean(centred * centred, -1, keepdims=True)
    return centred * lax.rsqrt(variance + norm_eps)


def split_pair(values):
    high = values.astype(bf16)
    return high, (values - high.astype(f32)).astype(bf16)


def dot(a, b):
    return jnp.dot(a, b, preferred_element_type=f32)


def dot_t(a, b):
    return lax.dot_general(a, b, (((1,), (1,)), ((), ())), preferred_element_type=f32)


def kernel(
    sizes,
    hidden_hbm,
    now_hbm,
    next_hbm,
    step_hbm,
    tag_hbm,
    level_hbm,
    final_hbm,
    time_hbm,
    sqkv_hbm,
    sout_hbm,
    tqkv_hbm,
    tout_hbm,
    logp_ref,
    mean_ref,
    step_ref,
    tag_ref,
    level_ref,
    hidden_ref,
    now_ref,
    next_ref,
    final_ref,
    time_w,
    sqkv_w,
    sout_w,
    tqkv_w,
    tout_w,
    table,
    group_ref,
    spread_ref,
    mask_ref,
    after_ref,
    q_ref,
    k_ref,
    v_ref,
    out_buf,
    in_buf,
    back_buf,
    ret_buf,
    w_sem,
    send_sem,
    recv_sem,
    send2_sem,
    recv2_sem,
):
    inner_size, outer_size = sizes
    peers = inner_size * outer_size
    rows, width = hidden_hbm.shape
    count = rows // peers
    chunks = 2 if inner_size % 2 == 0 else 1
    halves = 2 if outer_size % 2 == 0 else 1
    span = outer_size // halves
    block_peers = peers // halves
    size = rows // chunks
    part = rows // halves
    each = inner_size // chunks
    head = width // HEADS
    channels = final_hbm.shape[0]
    tiles = width // LANES
    inner = lax.axis_index("inner")
    outer = lax.axis_index("outer")
    me = inner * outer_size + outer
    core = lax.rem(inner, chunks)

    side = outer // span

    def slot_of(inner_id, outer_id):
        return outer_id * inner_size + inner_id

    def block_of(inner_id, outer_id):
        return (lax.rem(inner_id, chunks) * outer_size + outer_id) * each + inner_id // chunks

    my_slot = slot_of(inner, outer)
    my_block = block_of(inner, outer)

    early = -(-tiles // 2) * LANES

    def fetch(source, target, index, lo, hi):
        return pltpu.make_async_copy(
            source.at[:, lo:hi], target.at[:, lo:hi], w_sem.at[index]
        )

    loads = [
        fetch(time_hbm, time_w, 0, 0, 2 * width),
        fetch(sqkv_hbm, sqkv_w, 1, width, width + early),
        fetch(sqkv_hbm, sqkv_w, 2, 2 * width, 3 * width),
        fetch(sqkv_hbm, sqkv_w, 3, 0, width),
        fetch(time_hbm, time_w, 4, 2 * width, 3 * width),
        fetch(sout_hbm, sout_w, 5, 0, width),
        fetch(tqkv_hbm, tqkv_w, 6, 0, 3 * width),
        fetch(tout_hbm, tout_w, 7, 0, width),
        fetch(sqkv_hbm, sqkv_w, 15, width + early, 2 * width),
        fetch(time_hbm, time_w, 16, 3 * width, 6 * width),
    ]
    rest = [
        pltpu.make_async_copy(now_hbm, now_ref, w_sem.at[9]),
        pltpu.make_async_copy(next_hbm, next_ref, w_sem.at[10]),
        pltpu.make_async_copy(final_hbm, final_ref, w_sem.at[11]),
        pltpu.make_async_copy(tag_hbm, tag_ref, w_sem.at[12]),
        pltpu.make_async_copy(level_hbm, level_ref, w_sem.at[13]),
    ]
    hidden_load = pltpu.make_async_copy(hidden_hbm, hidden_ref, w_sem.at[8])
    step_load = pltpu.make_async_copy(step_hbm, step_ref, w_sem.at[14])
    step_load.start()
    hidden_load.start()
    loads[0].start()
    for index in (1, 8, 2, 3, 5, 4, 6, 7, 9):
        loads[index].start()
    for load in rest:
        load.start()

    barrier = pltpu.get_barrier_semaphore()

    def wrap(value, bound):
        return jnp.where(value >= bound, value - bound, value)

    for turn in range(outer_size):
        to_outer = wrap(outer + turn, outer_size)

        @pl.loop(1 if turn == 0 else 0, inner_size)
        def _(k):
            pl.semaphore_signal(
                barrier,
                inc=1,
                device_id=(wrap(inner + k, inner_size), to_outer),
                device_id_type=MESH,
            )

    feature = lax.broadcasted_iota(jnp.int32, (width, LANES), 0)
    column = lax.broadcasted_iota(jnp.int32, (width, LANES), 1) * head
    group_ref[...] = jnp.where(
        (feature >= column) & (feature < column + head), 1.0, 0.0
    ).astype(bf16)
    feature = lax.broadcasted_iota(jnp.int32, (LANES, width), 1)
    column = lax.broadcasted_iota(jnp.int32, (LANES, width), 0) * head
    spread = jnp.where((feature >= column) & (feature < column + head), 1.0, 0.0).astype(bf16)
    spread_ref[0:LANES, :] = spread
    spread_ref[LANES:, :] = spread

    step_load.wait()
    time_value = jnp.full((8, LANES), step_ref[0].astype(f32)) / STEPS
    lane = lax.broadcasted_iota(jnp.int32, (8, LANES), 1).astype(f32)
    angles = 1000.0 * time_value * jnp.exp(-math.log(10000.0) * lane / LANES)
    embedded = jnp.concatenate([jnp.cos(angles), jnp.sin(angles)], 1)
    activated = (embedded / (1.0 + jnp.exp(-embedded))).astype(bf16)
    hidden_load.wait()
    standard = layer_norm(hidden_ref[...].astype(f32))
    loads[0].wait()
    table[:, 0 : 2 * width] = dot(activated, time_w[:, 0 : 2 * width])

    def entry(index):
        return table[0:1, index * width : (index + 1) * width]

    normed = (standard * (1.0 + entry(1)) + entry(0)).astype(bf16)

    def head_norm_both(queries, keys):
        both = jnp.concatenate([queries, keys], 0)
        total = dot((both * both).astype(bf16), group_ref[...])
        inverse = lax.rsqrt(total / head + norm_eps)
        cut = queries.shape[0]
        inverse = jnp.concatenate([inverse[:cut] * head**-0.5, inverse[cut:]], 0)
        high, low = split_pair(inverse)
        both = (both * dot(jnp.concatenate([high, low], 1), spread_ref[...])).astype(bf16)
        return both[:cut], both[cut:]

    def head_norm(values, factor):
        total = dot((values * values).astype(bf16), group_ref[...])
        inverse = lax.rsqrt(total / head + norm_eps) * factor
        high, low = split_pair(inverse)
        return (values * dot(jnp.concatenate([high, low], 1), spread_ref[...])).astype(bf16)

    lane_id = lax.broadcasted_iota(jnp.int32, (1, WINDOW), 1)

    def own_lanes(index, tile):
        inside = (lane_id >= index * head - tile * LANES) & (
            lane_id < (index + 1) * head - tile * LANES
        )
        return jnp.where(inside, 1.0, 0.0).astype(bf16)

    def window_of(index):
        tile = min(index * head // LANES, (width - WINDOW) // LANES)
        return tile, slice(tile * LANES, tile * LANES + WINDOW)

    def attend(queries, masked):
        tops, bottoms = [None] * tiles, [None] * tiles
        for first in range(0, HEADS, GROUP):
            group = range(first, first + GROUP)
            scores = []
            for index in range(first, first + GROUP, 2):
                tile, window = window_of(index)
                query = queries[:, window]
                pair = [query * own_lanes(index + turn, tile) for turn in range(2)]
                score = dot_t(jnp.concatenate(pair, 0), k_ref[:, window])
                scores += [score[: query.shape[0]], score[query.shape[0] :]]
            weights = [jnp.exp(score).astype(bf16) for score in scores]
            if masked:
                weights = [weight * mask_ref[...] for weight in weights]
            for index, weight in zip(group, weights):
                tile, window = window_of(index)
                own = own_lanes(index, tile)
                mixed = dot(weight, jnp.where(own > 0.5, v_ref[:, window], own + 1.0))
                for side in range(WINDOW // LANES):
                    begin = index * head - (tile + side) * LANES
                    if begin >= LANES or begin + head <= 0:
                        continue
                    top = mixed[:, side * LANES : (side + 1) * LANES]
                    bottom = mixed[:, (1 - side) * LANES : (2 - side) * LANES]
                    here = tile + side
                    if tops[here] is None:
                        tops[here], bottoms[here] = top, bottom
                    else:
                        short = lane_id[:, :LANES] >= begin
                        tops[here] = jnp.where(short, top, tops[here])
                        bottoms[here] = jnp.where(short, bottom, bottoms[here])
        return jnp.concatenate(
            [(top / bottom).astype(bf16) for top, bottom in zip(tops, bottoms)], 1
        )

    loads[1].wait()
    first = dot(normed, sqkv_w[:, width : width + early])
    loads[8].wait()
    second = dot(normed, sqkv_w[:, width + early : 2 * width])
    k_ref[...] = head_norm(jnp.concatenate([first, second], 1), 1.0)
    loads[2].wait()
    v_ref[...] = dot(normed, sqkv_w[:, 2 * width : 3 * width]).astype(bf16)
    loads[3].wait()

    def forward(inner_id, outer_id, chunk, turn):
        return pltpu.make_async_remote_copy(
            src_ref=out_buf.at[block_of(inner_id, outer_id)],
            dst_ref=in_buf.at[my_slot],
            send_sem=send_sem.at[chunk, turn],
            recv_sem=recv_sem.at[outer],
            device_id=(inner_id, outer_id),
            device_id_type=MESH,
        )

    def backward(inner_id, outer_id, turn):
        return pltpu.make_async_remote_copy(
            src_ref=back_buf.at[slot_of(inner_id, outer_id)],
            dst_ref=ret_buf.at[my_block],
            send_sem=send2_sem.at[turn],
            recv_sem=recv2_sem.at[turn],
            device_id=(inner_id, outer_id),
            device_id_type=MESH,
        )

    def partners(turn):
        return block_peers - (1 if turn == halves - 1 else 0)

    def several(source, target, sends, receives, blocks):
        return pltpu.make_async_remote_copy(
            src_ref=source.at[pl.ds(0, blocks)],
            dst_ref=target.at[pl.ds(0, blocks)],
            send_sem=sends,
            recv_sem=receives,
            device_id=(inner, outer),
            device_id_type=MESH,
        )

    def half_of(turn):
        return lax.rem(side + 1 + turn, halves)

    place = outer - side * span

    def send(chunk, turn):
        for step in range(span):
            to_outer = half_of(turn) * span + wrap(place + step, span)

            def start(k):
                to_inner = wrap(inner // chunks + k, each) * chunks + chunk
                forward(to_inner, to_outer, chunk, turn).start()

            if turn == halves - 1 and step == 0:

                @pl.when(core != chunk)
                def _():
                    start(0)

                pl.loop(1, each, unroll=True)(start)
            else:
                pl.loop(0, each, unroll=True)(start)

    for chunk in range(chunks):
        lo = chunk * size
        queries = head_norm(dot(normed[lo : lo + size], sqkv_w[:, 0:width]), head**-0.5)
        attended = attend(queries, False)
        if chunk == 0:
            loads[5].wait()
            loads[4].wait()
            table[:, 2 * width : 3 * width] = dot(activated, time_w[:, 2 * width : 3 * width])
        projected = dot(attended, sout_w[...])
        after = hidden_ref[lo : lo + size, :].astype(f32) + entry(2) * projected
        out_buf[chunk * outer_size * each : (chunk + 1) * outer_size * each] = after.reshape(
            outer_size * each, count, width
        ).astype(bf16)
        if chunk == 0:
            pl.semaphore_wait(barrier, peers - 1)
        for turn in range(halves) if chunk == 0 else reversed(range(halves)):
            send(chunk, turn)
    in_buf[my_slot] = out_buf[my_block]

    loads[9].wait()
    table[:, 3 * width :] = dot(activated, time_w[:, 3 * width :])
    row = lax.rem(lax.broadcasted_iota(jnp.int32, (rows, rows), 0), count)
    other = lax.rem(lax.broadcasted_iota(jnp.int32, (rows, rows), 1), count)
    mask_ref[...] = jnp.where(row == other, 1.0, 0.0).astype(bf16)
    slot = lax.rem(lax.broadcasted_iota(jnp.int32, (rows, LANES), 0), count)
    own_slot = slot == lax.broadcasted_iota(jnp.int32, (rows, LANES), 1) // channels
    loads[6].wait()
    loads[7].wait()
    for load in rest:
        load.wait()
    repeated = jnp.concatenate([final_ref[...]] * (LANES // channels), 0)

    stages = [[side * span + step for step in range(span)]]
    if halves == 2:
        for step in range(span):
            stages.append([jnp.where(side == 0, outer_size - 1 - step, step)])

    def arrive(outer_id):
        def wait(blocks):
            several(
                out_buf, in_buf, send_sem.at[0, 0], recv_sem.at[outer_id], blocks
            ).wait_recv()

        pl.when(outer_id == outer)(lambda: wait(inner_size - 1))
        pl.when(outer_id != outer)(lambda: wait(inner_size))

    def enter(outer_ids, lo):
        pieces = []
        for outer_id in outer_ids:
            arrive(outer_id)
            piece = in_buf[pl.ds(outer_id * inner_size, inner_size)]
            pieces.append(piece.astype(f32).reshape(inner_size * count, width))
        after = jnp.concatenate(pieces, 0)
        hi = lo + after.shape[0]
        normed = (layer_norm(after) * (1.0 + entry(4)) + entry(3)).astype(bf16)
        after_ref[lo:hi, :] = after.astype(bf16)
        mixed = dot(normed, tqkv_w[:, 0 : 2 * width])
        q_ref[lo:hi, :], k_ref[lo:hi, :] = head_norm_both(mixed[:, :width], mixed[:, width:])
        v_ref[lo:hi, :] = dot(normed, tqkv_w[:, 2 * width :]).astype(bf16)

    enter(stages[0], 0)
    if halves == 2:
        rim = (outer == 0) | (outer == outer_size - 1)
        distant = [stage[0] for stage in stages[1:]]

        @pl.when(rim)
        def _():
            enter(distant, span * inner_size * count)

        @pl.when(jnp.logical_not(rim))
        def _():
            for step in range(span):
                enter(distant[step : step + 1], (span + step) * inner_size * count)

    attended = attend(q_ref, True)
    term = dot(attended, tout_w[...]).astype(bf16).astype(f32)
    final_normed = layer_norm(after_ref[...].astype(f32) + entry(5) * term).astype(bf16)
    mixed = jnp.where(own_slot, dot_t(final_normed, repeated), 0.0)
    packed = jnp.sum(mixed.reshape(peers, count, LANES), 1)
    packed = packed.reshape(peers, 1, LANES)
    done = 0
    for stage in stages:
        blocks = len(stage) * inner_size
        back_buf[pl.ds(stage[0] * inner_size, blocks)] = packed[done : done + blocks]
        done += blocks
    for turn in range(halves):

        for step in range(span):
            to_outer = half_of(turn) * span + wrap(place + step, span)

            @pl.loop(1 if turn == halves - 1 and step == 0 else 0, inner_size, unroll=True)
            def _(k):
                backward(wrap(inner + k, inner_size), to_outer, turn).start()

    ret_buf[my_block] = back_buf[my_slot]

    level = jnp.float32(0.0)
    for version in range(level_ref.shape[0]):
        level = level + jnp.where(tag_ref[0] == version, level_ref[version], 0.0)
    time_row = jnp.full((1, rows), step_ref[0].astype(f32)) / STEPS
    noise_scale = level * jnp.sqrt(time_row / (1.0 - time_row))
    factor = noise_scale * noise_scale / (2.0 * time_row)
    deviation = noise_scale * math.sqrt(1.0 / STEPS)
    lane = lax.broadcasted_iota(jnp.int32, (channels, LANES), 1)
    pick = lax.rem(lane, channels) == lax.broadcasted_iota(jnp.int32, (channels, LANES), 0)
    pick = jnp.where(pick, 1.0, 0.0).astype(bf16)
    for chunk in range(chunks):
        for turn in range(halves - 1):
            several(out_buf, in_buf, send_sem.at[chunk, turn], recv_sem.at[0], span * each).wait_send()
        last = halves - 1

        @pl.when(core != chunk)
        def _():
            several(out_buf, in_buf, send_sem.at[chunk, last], recv_sem.at[0], span * each).wait_send()

        @pl.when(core == chunk)
        def _():
            several(out_buf, in_buf, send_sem.at[chunk, last], recv_sem.at[0], span * each - 1).wait_send()

    for turn in range(halves):
        several(
            back_buf, ret_buf, send2_sem.at[turn], recv2_sem.at[turn], partners(turn)
        ).wait_recv()
    packed = jnp.broadcast_to(ret_buf[...], (peers, count, LANES)).reshape(rows, LANES)
    packed = jnp.where(own_slot, packed, 0.0)
    high = packed.astype(bf16)
    residue = packed - high.astype(f32)
    middle = residue.astype(bf16)
    low = (residue - middle.astype(f32)).astype(bf16)
    velocity = dot_t(pick, high) + dot_t(pick, middle) + dot_t(pick, low)
    now = now_ref[0]
    drift = velocity + factor * (now + (1.0 - time_row) * velocity)
    next_mean = now - drift / STEPS
    mean_ref[0] = next_mean
    standard = (next_ref[0] - next_mean) / deviation
    logp_ref[...] = (
        -0.5 * jnp.mean(standard * standard, 0, keepdims=True)
        - jnp.log(deviation)
        - 0.5 * math.log(2.0 * math.pi)
    )
    for turn in range(halves):
        several(
            back_buf, ret_buf, send2_sem.at[turn], recv2_sem.at[turn], partners(turn)
        ).wait_send()


def shards(sizes, hidden, now, following, step, tags, levels, time_w, sqkv, sout, tqkv, tout, final):
    peers = sizes[0] * sizes[1]
    rows, width = hidden.shape
    count = rows // peers
    vmem = pl.BlockSpec(memory_space=pltpu.VMEM)
    hbm = pl.BlockSpec(memory_space=pl.ANY)
    exchange = pltpu.VMEM((peers, count, width), bf16)
    returned = pltpu.VMEM((peers, 1, LANES), f32)
    sems = pltpu.SemaphoreType.DMA((2,))
    arrivals = pltpu.SemaphoreType.DMA((sizes[1],))
    return pl.pallas_call(
        functools.partial(kernel, sizes),
        out_shape=(pltpu.VMEM((1, rows), f32), pltpu.VMEM(now.shape, f32)),
        in_specs=[hbm] * 12,
        out_specs=(vmem, vmem),
        scratch_shapes=[
            pltpu.SMEM(step.shape, step.dtype),
            pltpu.SMEM(tags.shape, tags.dtype),
            pltpu.SMEM(levels.shape, levels.dtype),
            pltpu.VMEM(hidden.shape, bf16),
            pltpu.VMEM(now.shape, f32),
            pltpu.VMEM(following.shape, f32),
            pltpu.VMEM(final.shape, bf16),
            pltpu.VMEM(time_w.shape, bf16),
            pltpu.VMEM(sqkv.shape, bf16),
            pltpu.VMEM(sout.shape, bf16),
            pltpu.VMEM(tqkv.shape, bf16),
            pltpu.VMEM(tout.shape, bf16),
            pltpu.VMEM((8, 6 * width), f32),
            pltpu.VMEM((width, LANES), bf16),
            pltpu.VMEM((2 * LANES, width), bf16),
            pltpu.VMEM((rows, rows), bf16),
            pltpu.VMEM((rows, width), bf16),
            pltpu.VMEM((rows, width), bf16),
            pltpu.VMEM((rows, width), bf16),
            pltpu.VMEM((rows, width), bf16),
            exchange,
            exchange,
            returned,
            returned,
            pltpu.SemaphoreType.DMA((17,)),
            pltpu.SemaphoreType.DMA((2, 2)),
            arrivals,
            sems,
            sems,
        ],
        compiler_params=pltpu.CompilerParams(
            collective_id=0, has_side_effects=True, vmem_limit_bytes=60 * 1024 * 1024
        ),
    )(hidden, now, following, step, tags, levels, final, time_w, sqkv, sout, tqkv, tout)


def solution(mesh):
    split = P(("inner", "outer"), None)
    split3 = P(("inner", "outer"), None, None)
    sizes = (mesh.shape["inner"], mesh.shape["outer"])
    return jax.shard_map(
        functools.partial(shards, sizes),
        mesh=mesh,
        in_specs=(split, split3, split3, P(), P(("inner", "outer")))
        + (P(),) * 7,
        out_specs=(split, split3),
        check_vma=False,
    )
```
